32 devices in a mesh: dp: 4 (over z), section: 2 (over x), mp: 4 (over y, core).
Axes of the slice: x: 2, y: 2, z: 4, core: 2. Of those that a mesh axis runs over, the one named last changes fastest.
Arguments:
- source_rows: bfloat16 [1024, 1024], P('dp', 'mp'), may hold values from -6 to 6
- value_weight: bfloat16 [2, 1024, 1024], P('section', None, 'mp'), may hold values from -0.1875 to 0.1875
- gate_weight: bfloat16 [2, 1024, 1024], P('section', None, 'mp'), may hold values from -0.1875 to 0.1875
- kernel_weight: bfloat16 [2, 1024, 496], P('section', None, 'mp'), may hold values from -0.1875 to 0.1875
- segment_ids: int32 [8, 128], P('dp'), may hold values from 0 to 3, never falling along the last dimension, each value on 1 to 64 neighbouring positions
- out_grad: bfloat16 [1024, 1024], P('dp', 'mp'), may hold values from -6 to 6
Outputs:
- value_grad: float32 [2, 1024, 1024], P('section', 'dp', 'mp')
- gate_grad: float32 [2, 1024, 1024], P('section', 'dp', 'mp')
- kernel_grad: float32 [2, 1024, 496], P('section', 'dp', 'mp')
The draws below stay inside these ranges and needn't reach their ends.
Inputs may be any that keep to these rules, and one draw needn't show every extreme that they name: `segment_ids`: in each microbatch row of 128 positions the sentence numbers never fall and every number from 0 up to the largest appears; a sentence covers 1 to 64 positions, and in every microbatch exactly one sentence covers 64 positions.
All inputs are finite; a program needn't handle non-finite values.
Results may differ from the reference program's by a relative error of at most 0.015.
Values may be sent and summed in bfloat16 or wider, within the bound.
A program may use at most 64 MiB of HBM per device.

```python
import math
import jax
import jax.numpy as jnp
import numpy as np
from jax import lax

D = 1024
HEADS = 16
KERNEL = 31
ROWS = 128
MICRO = 2
LAYERS = 2
TOKENS = 1024
N_DP = 4


def strengthened(drawn, key, source, target, shards_of, factor):
    owner, partner = [(jnp.arange(drawn.shape[axis_at]) // (drawn.shape[axis_at] // shards_of)).reshape([-1 if axis == axis_at else 1 for axis in range(drawn.ndim)]) for axis_at in (source, target)]
    chosen = jax.random.permutation(key, shards_of)[partner]
    strong = (owner == chosen) | (owner == (partner + shards_of // 2) % shards_of)
    return jnp.where(strong, factor * drawn, drawn)


def block_levels(own_key, shape, cuts, low, largest):
    def one(dim, parts):
        draws = jax.random.uniform(jax.random.fold_in(jax.random.fold_in(own_key, 6), dim), (parts,), jnp.float32, low / len(cuts), largest / len(cuts))
        return jnp.repeat(jnp.exp(draws), shape[dim] // parts).reshape((-1,) + (1,) * (len(shape) - dim - 1))

    level = one(*cuts[0])
    for cut in cuts[1:]:
        level = level * one(*cut)
    return level


def split_up(amount, total, bound, skew):
    portions = [(1 << 20) // math.isqrt(grade ** skew) + 1 for grade in range(2, amount + 1)]
    surplus, given = total - bound - (amount - 1), [1] * (amount - 1)
    while surplus > 0:
        movable = [i for i in range(amount - 1) if given[i] < bound]
        pool, left = sum([portions[i] for i in movable]), surplus
        for i in movable:
            addition = min(bound - given[i], max(1, left * portions[i] // pool), surplus)
            given[i] = given[i] + addition
            surplus = surplus - addition
    return np.array([bound] + given)


def ragged(rng, count, total, most, slope):
    if count == 2:
        one = jax.random.randint(rng, (), max(1, total - most), min(most, total - 1) + 1)
        return jnp.stack([one, total - one])
    tallies = jnp.asarray(split_up(count, total, most, slope), jnp.int32)
    twos = (count - 1) // 2
    source_of, receiver = tallies[1:1 + 2 * twos:2], tallies[2:2 + 2 * twos:2]
    room = jnp.minimum(source_of - 1, most - receiver)
    moved = jax.random.randint(jax.random.fold_in(rng, 1), (twos,), 0, 1 << 20) % (room + 1)
    tallies = tallies.at[1:1 + 2 * twos:2].set(source_of - moved).at[2:2 + 2 * twos:2].set(receiver + moved)
    return tallies[jax.random.permutation(jax.random.fold_in(rng, 2), count)]


def noise(own_key, shape, width, limit, cuts=(), held_as=jnp.bfloat16):
    drawn = jax.random.normal(own_key, shape, jnp.float32) * width
    if len(cuts) > 0:
        drawn = block_levels(own_key, shape, cuts, -0.22, 0.18) * drawn
    return jnp.clip(drawn, min=-limit, max=limit).astype(held_as)


def noise_with(stream_key, shape, scale, most, split, heavy, kind=jnp.bfloat16):
    drawn = scale * jax.random.normal(stream_key, shape, jnp.float32)
    if split:
        drawn = drawn * block_levels(stream_key, shape, split, -0.22, 0.18)
    return jnp.clip(strengthened(drawn, jax.random.fold_in(stream_key, 3), *heavy), -most, most).astype(kind)


def setup_inputs(seed: int = 0) -> dict:
    key_list = jax.random.split(jax.random.key(seed), 7)
    return {
        "source_rows": noise_with(key_list[0], (TOKENS, D), 1.0, 6.0, ((0, 4), (1, 4)), (0, 1, 4, 2.0)),
        "value_weight": noise(key_list[1], (LAYERS, D, D), D ** -0.5, 0.1875, ((0, 2), (2, 4))),
        "gate_weight": noise(key_list[2], (LAYERS, D, D), D ** -0.5, 0.1875, ((0, 2), (2, 4))),
        "kernel_weight": noise(key_list[3], (LAYERS, D, HEADS * KERNEL), D ** -0.5, 0.1875, ((0, 2), (2, 4))),
        "segment_ids": jax.vmap(lambda own: jnp.searchsorted(jnp.cumsum(ragged(own, max(3, ROWS // 32), ROWS, ROWS // 2, 2)), jnp.arange(ROWS), side="right"))(jax.random.split(key_list[4], (TOKENS // ROWS))).reshape((TOKENS // ROWS, ROWS)).astype(jnp.int32),
        "out_grad": noise(key_list[5], (TOKENS, D), 1.0, 6.0, ((0, 4), (1, 4))),
    }


def make_table(segments):
    row_count = segments.shape[0]
    positions = jnp.arange(row_count, dtype=jnp.int32)
    offsets = positions[None, :] - positions[:, None] + KERNEL // 2
    same_doc = segments[:, None] == segments[None, :]
    tap_index = jnp.arange(KERNEL, dtype=jnp.int32)[:, None, None]
    return ((offsets[None] == tap_index) & same_doc[None]).astype(jnp.float32)

def rounded(values):
    return lax.optimization_barrier(values.astype(jnp.bfloat16)).astype(jnp.float32)

def normalize(rows_in):
    widened = rows_in.astype(jnp.float32)
    row_mean = lax.optimization_barrier(jnp.mean(widened, axis=-1, keepdims=True))
    centred = widened - row_mean
    inv_std = lax.rsqrt(lax.optimization_barrier(jnp.mean(centred * centred, axis=-1, keepdims=True)) + 1e-05)
    normed = centred * inv_std
    return (normed, inv_std, normed.astype(jnp.bfloat16))

def forward_pieces(normed_b, band_table, w_value, w_gate, w_kernel):
    row_count = normed_b.shape[0]
    value_proj = jnp.dot(normed_b, w_value, preferred_element_type=jnp.float32)
    gate_proj = jnp.dot(normed_b, w_gate, preferred_element_type=jnp.float32)
    gate_sig = jax.nn.sigmoid(gate_proj)
    gated = rounded(value_proj * gate_sig)
    head_count = w_kernel.shape[1] // KERNEL
    head_size = w_value.shape[1] // head_count
    logits = jnp.dot(normed_b, w_kernel, preferred_element_type=jnp.float32).reshape(row_count, head_count, KERNEL)
    exp_logits = jnp.exp(logits)
    taps = exp_logits / lax.optimization_barrier(jnp.sum(exp_logits, axis=-1, keepdims=True))
    band_mat = jnp.einsum('thj,jts->hts', rounded(taps), band_table)
    gated3 = gated.reshape(row_count, head_count, head_size)
    mixed = jnp.einsum('hts,shd->thd', band_mat, gated3).reshape(row_count, -1)
    return (value_proj, gate_sig, gated3, taps, band_mat, mixed)

def backward_pieces(normed_b, band_table, grad_out, w_value, w_gate, w_kernel):
    value_proj, gate_sig, gated3, taps, band_mat, mixed = forward_pieces(normed_b, band_table, w_value, w_gate, w_kernel)
    row_count, head_count, head_size = gated3.shape
    grad_mixed = rounded(grad_out).reshape(row_count, head_count, head_size)
    grad_gated = jnp.einsum('hts,thd->shd', band_mat, grad_mixed).reshape(row_count, -1)
    tap_outer = jnp.einsum('thd,shd->hts', grad_mixed, gated3)
    grad_taps = jnp.einsum('hts,jts->thj', tap_outer, band_table)
    grad_logits = (taps * (grad_taps - lax.optimization_barrier(jnp.sum(taps * grad_taps, axis=-1, keepdims=True)))).astype(jnp.bfloat16).reshape(row_count, -1)
    grad_value = (grad_gated * gate_sig).astype(jnp.bfloat16)
    grad_gate = (grad_gated * value_proj * gate_sig * (1.0 - gate_sig)).astype(jnp.bfloat16)
    dims = (((1,), (1,)), ((), ()))
    grad_normed = lax.dot_general(grad_value, w_value, dims, preferred_element_type=jnp.float32)
    grad_normed = grad_normed + lax.dot_general(grad_gate, w_gate, dims, preferred_element_type=jnp.float32)
    grad_normed = grad_normed + lax.dot_general(grad_logits, w_kernel, dims, preferred_element_type=jnp.float32)
    return (grad_normed, grad_value, grad_gate, grad_logits)

def outer_sum(normed_b, grad_rows):
    return lax.dot_general(normed_b, grad_rows, (((0,), (0,)), ((), ())), preferred_element_type=jnp.float32)

def reference(source_rows, value_weight, gate_weight, kernel_weight, segment_ids, out_grad):
    sources = source_rows.reshape(N_DP, MICRO, ROWS, D)
    cotangents = out_grad.reshape(N_DP, MICRO, ROWS, D)
    segments_all = segment_ids.reshape(N_DP, MICRO, ROWS)
    kernel_cols = HEADS * KERNEL

    def micro_step(accumulated, entry):
        rows_in, top_grad, segments = entry
        band_table = make_table(segments)
        hidden = rows_in
        layer_inputs = []
        for layer_no in range(LAYERS):
            layer_inputs.append(hidden)
            normed, inv_std, normed_b = normalize(hidden)
            pieces = forward_pieces(normed_b, band_table, value_weight[layer_no], gate_weight[layer_no], kernel_weight[layer_no])
            hidden = (hidden.astype(jnp.float32) + pieces[5]).astype(jnp.bfloat16)
        sums_value, sums_gate, sums_kernel = accumulated
        grad_out = top_grad.astype(jnp.float32)
        for layer_no in reversed(range(LAYERS)):
            normed, inv_std, normed_b = normalize(layer_inputs[layer_no])
            grad_normed, grad_value, grad_gate, grad_logits = backward_pieces(normed_b, band_table, grad_out, value_weight[layer_no], gate_weight[layer_no], kernel_weight[layer_no])
            sums_value = sums_value.at[layer_no].add(outer_sum(normed_b, grad_value))
            sums_gate = sums_gate.at[layer_no].add(outer_sum(normed_b, grad_gate))
            sums_kernel = sums_kernel.at[layer_no].add(outer_sum(normed_b, grad_logits))
            norm_back = inv_std * (grad_normed - lax.optimization_barrier(jnp.mean(grad_normed, axis=-1, keepdims=True)) - normed * lax.optimization_barrier(jnp.mean(grad_normed * normed, axis=-1, keepdims=True)))
            grad_out = grad_out + norm_back
        return ((sums_value, sums_gate, sums_kernel), None)

    def empty_sums():
        return (jnp.zeros((LAYERS, D, D), jnp.float32), jnp.zeros((LAYERS, D, D), jnp.float32), jnp.zeros((LAYERS, D, kernel_cols), jnp.float32))

    def replica_step(totals, entry):
        partials, unused = lax.scan(micro_step, empty_sums(), entry)
        merged = tuple((total + rounded(partial_value) for total, partial_value in zip(totals, partials)))
        return (merged, None)
    totals, unused = lax.scan(replica_step, empty_sums(), (sources, cotangents, segments_all))
    return (totals[0], totals[1], totals[2])
```

```python
import functools

import jax
import jax.numpy as jnp
from jax import lax
from jax.experimental import pallas as pl
from jax.experimental.pallas import tpu as pltpu
from jax.sharding import PartitionSpec as P

KERNEL = 31
MESH = pl.DeviceIdType.MESH
F32 = jnp.float32
BF16 = jnp.bfloat16


def remote(src, dst, send_sem, recv_sem, device):
    return pltpu.make_async_remote_copy(
        src_ref=src,
        dst_ref=dst,
        send_sem=send_sem,
        recv_sem=recv_sem,
        device_id=device,
        device_id_type=MESH,
    )


def dot(a, b):
    return jnp.dot(a, b, preferred_element_type=F32)


def dot_nt(a, b):
    return lax.dot_general(a, b, (((1,), (1,)), ((), ())), preferred_element_type=F32)


def dot_tn(a, b):
    return lax.dot_general(a, b, (((0,), (0,)), ((), ())), preferred_element_type=F32)


def skew(values, shift):
    fine = shift % 8
    if fine:
        values = pltpu.roll(values, fine, 1)
    return pltpu.roll(values, shift - fine, 1, stride=1, stride_axis=0)


def kernel(
    n_dp,
    micro,
    src_ref,
    wv_ref,
    wg_ref,
    wk_ref,
    seg_ref,
    og_ref,
    vout_ref,
    gout_ref,
    kout_ref,
    xall,
    nf,
    nb,
    invs,
    nt_full,
    nt_all,
    wkp,
    lgs,
    masks,
    vs,
    sigs,
    gateds,
    tps,
    bds,
    hs,
    gbuf,
    gs,
    terms,
    rs_buf,
    rs_in,
    st_buf,
    st_in,
    acc,
    ag_send,
    ag_recv,
    h_send,
    h_recv,
    nt_send,
    nt_recv,
    right_send,
    left_send,
    ring_recv,
    rs_send,
    rs_recv,
    st_send,
    st_recv,
    g_send,
    g_recv,
):
    d = lax.axis_index("dp")
    s = lax.axis_index("section")
    m = lax.axis_index("mp")
    near = m + 1 - 2 * lax.rem(m, 2)
    across = lax.rem(m + 2, 4)
    corner = lax.rem(near + 2, 4)
    partners = (near, across, corner)
    other = {"section": 1 - s}
    rows = seg_ref.shape[1]
    width = wv_ref.shape[2]
    full = wv_ref.shape[1]
    kcols = wk_ref.shape[2]
    heads = kcols // KERNEL
    n_mp = full // width
    slab = full // n_dp
    micros = range(micro)

    lanes = lax.broadcasted_iota(jnp.int32, (rows, rows), 1)
    subs = lax.broadcasted_iota(jnp.int32, (rows, rows), 0)
    offset = lanes - subs + KERNEL // 2
    cyclic = lax.rem(offset + rows, rows) < KERNEL
    low_half = lanes < rows // 2
    flip = jnp.where(lanes + subs == rows - 1, 1.0, 0.0).astype(BF16)

    barrier = pltpu.get_barrier_semaphore()
    for p in partners:
        pl.semaphore_signal(barrier, inc=1, device_id={"mp": p}, device_id_type=MESH)
    pl.semaphore_signal(barrier, inc=1, device_id=other, device_id_type=MESH)

    def greet(i, carry):
        pl.semaphore_signal(
            barrier, inc=1, device_id={"dp": lax.rem(d + i, n_dp)}, device_id_type=MESH
        )
        return carry

    lax.fori_loop(1, n_dp, greet, 0)

    @pl.when(s == 0)
    def _():
        for mb in micros:
            xall[mb, m] = src_ref[mb * rows : (mb + 1) * rows, :]

    @pl.when(s == 1)
    def _():
        for mb in micros:
            gbuf[mb] = og_ref[mb * rows : (mb + 1) * rows, :]

    pl.semaphore_wait(barrier, 4 + n_dp - 1)

    def gather_copy(mb, rel):
        block = (m, m, across)[rel]
        target = (near, across, near)[rel]
        return remote(
            xall.at[mb, block],
            xall.at[mb, block],
            ag_send.at[mb, rel],
            ag_recv.at[mb, rel],
            {"mp": target},
        )

    def gather_wait(mb, rel):
        block = (near, across, corner)[rel]
        remote(
            xall.at[mb, block],
            xall.at[mb, block],
            ag_send.at[mb, rel],
            ag_recv.at[mb, rel],
            {"mp": near},
        ).wait_recv()

    def h_copy(mb):
        return remote(hs.at[mb], xall.at[mb, m], h_send.at[mb], h_recv.at[mb], other)

    def g_copy(mb):
        return remote(gs.at[mb], gbuf.at[mb], g_send.at[mb], g_recv.at[mb], other)

    @pl.when(s == 0)
    def _():
        for mb in micros:
            gather_copy(mb, 1).start()
            gather_copy(mb, 0).start()

    wkp[...] = jnp.zeros_like(wkp)
    wkp[:, :kcols] = wk_ref[0]
    lgs[...] = jnp.zeros_like(lgs)
    acc[...] = jnp.zeros_like(acc)
    for mb in micros:
        across_seg = jnp.broadcast_to(seg_ref[mb : mb + 1, :].astype(F32), (rows, rows))
        down_seg = jnp.transpose(across_seg)
        same = (across_seg == down_seg) & (offset >= 0) & (offset < KERNEL)
        masks[mb] = jnp.where(same, 1.0, 0.0)

    def forward(mb):
        @pl.when(s == 1)
        def _():
            h_copy(mb).wait_recv()
            gather_copy(mb, 1).start()
            gather_copy(mb, 0).start()

        gather_wait(mb, 1)
        gather_copy(mb, 2).start()
        gather_wait(mb, 0)
        gather_wait(mb, 2)
        blocks = [xall[mb, j].astype(F32) for j in range(n_mp)]
        mean = sum(jnp.sum(b, axis=1, keepdims=True) for b in blocks) / full
        centred = [b - mean for b in blocks]
        var = sum(jnp.sum(c * c, axis=1, keepdims=True) for c in centred) / full
        inv = lax.rsqrt(var + 1e-05)
        invs[mb] = jnp.broadcast_to(inv, (rows, rows))
        for j in range(n_mp):
            normed = centred[j] * inv
            nf[mb, j] = normed
            nb[mb, :, j * width : (j + 1) * width] = normed.astype(BF16)
        normed_b = nb[mb]
        lgs[...] = dot(normed_b, wkp[...])
        value = dot(normed_b, wv_ref[0])
        sig = jax.nn.sigmoid(dot(normed_b, wg_ref[0]))
        vs[mb] = value
        sigs[mb] = sig
        gateds[mb] = (value * sig).astype(BF16)
        logits = lgs[...]
        in_band = masks[mb] > 0.0
        for h in range(heads):
            shift = (rows - KERNEL // 2 - KERNEL * h) % rows
            skewed = skew(logits, shift)
            weights = jnp.where(cyclic, jnp.exp(skewed), 0.0)
            taps = weights / jnp.sum(weights, axis=1, keepdims=True)
            tps[mb, h] = taps
            bds[mb, h] = jnp.where(in_band, taps, 0.0).astype(BF16)

        @pl.when(s == 0)
        def _():
            for p in range(heads // 2):
                cols = slice(p * rows, (p + 1) * rows)
                pair = gateds[mb, :, cols]
                mixed = jnp.where(
                    low_half, dot(bds[mb, 2 * p], pair), dot(bds[mb, 2 * p + 1], pair)
                )
                own = src_ref[mb * rows : (mb + 1) * rows, cols].astype(F32)
                hs[mb, :, cols] = (own + mixed).astype(BF16)
            h_copy(mb).start()

        for j in range(n_mp):
            nt_full[mb, j * width : (j + 1) * width, :] = jnp.transpose(nf[mb, j]).astype(BF16)

        def share(i, carry):
            k = lax.rem(d + i, n_dp)
            nt_copy(mb, k).start()
            return carry

        lax.fori_loop(1, n_dp, share, 0)
        nt_all[mb, d] = nt_full[mb, pl.ds(pl.multiple_of(d * slab, slab), slab), :]

    def nt_copy(mb, k):
        return remote(
            nt_full.at[mb, pl.ds(pl.multiple_of(k * slab, slab), slab), :],
            nt_all.at[mb, d],
            nt_send.at[mb, k],
            nt_recv.at[mb, d],
            {"dp": k},
        )

    def ring_copy(mb, k, step):
        sems = right_send if step == 1 else left_send
        return remote(
            terms.at[mb, k],
            terms.at[mb, k],
            sems.at[mb, k],
            ring_recv.at[mb, k],
            {"dp": d + step},
        )

    def ring_start(mb, k_right, k_left):
        @pl.when((d + 1 < n_dp) & (k_right >= 0))
        def _():
            ring_copy(mb, k_right, 1).start()

        @pl.when((d > 0) & (k_left < n_dp))
        def _():
            ring_copy(mb, k_left, -1).start()

    def backward(mb):
        @pl.when(s == 0)
        def _():
            g_copy(mb).wait_recv()

        in_band = masks[mb] > 0.0
        grad_logits = jnp.zeros((rows, rows), F32)
        for p in range(heads // 2):
            cols = slice(p * rows, (p + 1) * rows)
            grad_pair = gbuf[mb, :, cols]
            gated_pair = gateds[mb, :, cols]
            grad_gated = jnp.where(
                low_half,
                dot_tn(bds[mb, 2 * p], grad_pair),
                dot_tn(bds[mb, 2 * p + 1], grad_pair),
            )
            sig = sigs[mb, :, cols]
            grad_value = grad_gated * sig
            terms[mb, d, :, cols] = grad_value.astype(BF16)
            grad_gate = grad_value * vs[mb, :, cols] * (1.0 - sig)
            terms[mb, d, :, width + p * rows : width + (p + 1) * rows] = grad_gate.astype(BF16)
            for half in range(2):
                h = 2 * p + half
                keep = low_half if half == 0 else ~low_half
                part = jnp.where(keep, grad_pair.astype(F32), 0.0).astype(BF16)
                grad_taps = jnp.where(in_band, dot_nt(part, gated_pair), 0.0)
                taps = tps[mb, h]
                inner = jnp.sum(taps * grad_taps, axis=1, keepdims=True)
                skewed = (taps * (grad_taps - inner)).astype(BF16)
                shift = (KERNEL // 2 + KERNEL * h + 1) % rows
                grad_logits = grad_logits + skew(dot(flip, skewed), shift)
        terms[mb, d, :, 2 * width :] = dot(flip, grad_logits.astype(BF16)).astype(BF16)

        @pl.when(s == 0)
        def _():
            ring_start(mb, d, d)

        @pl.when(s == 1)
        def _():
            grad_value = terms[mb, d, :, :width]
            grad_gate = terms[mb, d, :, width : 2 * width]
            grad_log = terms[mb, d, :, 2 * width :]
            first = jnp.zeros((rows, 1), F32)
            second = jnp.zeros((rows, 1), F32)
            for j in range(n_mp):
                span = slice(j * width, (j + 1) * width)
                part = dot_nt(grad_value, wv_ref[0, span, :])
                part = part + dot_nt(grad_gate, wg_ref[0, span, :])
                part = part + dot_nt(grad_log, wkp[span, :])
                rs_buf[mb, j] = part.astype(BF16)
                first = first + jnp.sum(part, axis=1, keepdims=True)
                second = second + jnp.sum(part * nf[mb, j], axis=1, keepdims=True)
            both = jnp.transpose(jnp.where(lanes == 0, first, second))
            st_buf[mb] = both[:8]
            for rel in range(3):
                rs_copy(mb, rel).start()
                st_copy(mb, rel).start()
            ring_start(mb, d, d)

    def rs_copy(mb, rel):
        return remote(
            rs_buf.at[mb, partners[rel]],
            rs_in.at[mb, rel],
            rs_send.at[mb, rel],
            rs_recv.at[mb, rel],
            {"mp": partners[rel]},
        )

    def st_copy(mb, rel):
        return remote(
            st_buf.at[mb],
            st_in.at[mb, rel],
            st_send.at[mb, rel],
            st_recv.at[mb, rel],
            {"mp": partners[rel]},
        )

    def finish(mb):
        total = rs_buf[mb, m].astype(F32)
        stats = st_buf[mb]
        for rel in range(3):
            rs_copy(mb, rel).wait_recv()
            st_copy(mb, rel).wait_recv()
            total = total + rs_in[mb, rel].astype(F32)
            stats = stats + st_in[mb, rel]
        columns = jnp.transpose(stats) / full
        inv = invs[mb][:, :1]
        grad = inv * (total - columns[:, 0:1] - nf[mb, m] * columns[:, 1:2])
        gs[mb] = (gbuf[mb].astype(F32) + grad).astype(BF16)
        g_copy(mb).start()

    for mb in micros:
        forward(mb)
    for mb in micros:
        backward(mb)

        @pl.when(s == 1)
        def _():
            finish(mb)

    def accumulate(mb, k):
        acc[...] += dot(nt_all[mb, k], terms[mb, k])

    for mb in micros:
        accumulate(mb, d)

    def ring_step(i, carry):
        for mb in micros:
            left, right = d - i, d + i

            @pl.when(left >= 0)
            def _():
                ring_copy(mb, left, -1).wait_recv()

            @pl.when(right < n_dp)
            def _():
                ring_copy(mb, right, 1).wait_recv()

            ring_start(mb, left, right)
            for k, there in ((left, left >= 0), (right, right < n_dp)):

                @pl.when(there)
                def _():
                    remote(
                        nt_all.at[mb, k],
                        nt_all.at[mb, k],
                        nt_send.at[mb, k],
                        nt_recv.at[mb, k],
                        {"dp": k},
                    ).wait_recv()
                    accumulate(mb, k)

        return carry

    lax.fori_loop(1, n_dp, ring_step, 0)

    vout_ref[0] = acc[:, :width]
    gout_ref[0] = acc[:, width : 2 * width]
    kout_ref[0] = acc[:, 2 * width : 2 * width + kcols]

    for mb in micros:
        for rel in range(3):
            gather_copy(mb, rel).wait_send()

        @pl.when(s == 0)
        def _():
            h_copy(mb).wait_send()

        @pl.when(s == 1)
        def _():
            g_copy(mb).wait_send()
            for rel in range(3):
                rs_copy(mb, rel).wait_send()
                st_copy(mb, rel).wait_send()

        def drain(i, carry):
            @pl.when(i > 0)
            def _():
                nt_copy(mb, lax.rem(d + i, n_dp)).wait_send()

            @pl.when((d + 1 < n_dp) & (d - i >= 0))
            def _():
                ring_copy(mb, d - i, 1).wait_send()

            @pl.when((d > 0) & (d + i < n_dp))
            def _():
                ring_copy(mb, d + i, -1).wait_send()

            return carry

        lax.fori_loop(0, n_dp, drain, 0)


def shards(source_rows, value_weight, gate_weight, kernel_weight, segment_ids, out_grad):
    n_dp = lax.axis_size("dp")
    n_mp = lax.axis_size("mp")
    micro, rows = segment_ids.shape
    full, width = value_weight.shape[1:]
    kcols = kernel_weight.shape[2]
    heads = kcols // KERNEL
    slab = full // n_dp
    span = 2 * width + rows
    vmem = pl.BlockSpec(memory_space=pltpu.VMEM)
    dma = pltpu.SemaphoreType.DMA
    return pl.pallas_call(
        functools.partial(kernel, n_dp, micro),
        out_shape=(
            jax.ShapeDtypeStruct((1, slab, width), F32),
            jax.ShapeDtypeStruct((1, slab, width), F32),
            jax.ShapeDtypeStruct((1, slab, kcols), F32),
        ),
        in_specs=[vmem] * 6,
        out_specs=(vmem, vmem, vmem),
        scratch_shapes=[
            pltpu.VMEM((micro, n_mp, rows, width), BF16),
            pltpu.VMEM((micro, n_mp, rows, width), F32),
            pltpu.VMEM((micro, rows, full), BF16),
            pltpu.VMEM((micro, rows, rows), F32),
            pltpu.VMEM((micro, full, rows), BF16),
            pltpu.VMEM((micro, n_dp, slab, rows), BF16),
            pltpu.VMEM((full, rows), BF16),
            pltpu.VMEM((rows, rows), F32),
            pltpu.VMEM((micro, rows, rows), F32),
            pltpu.VMEM((micro, rows, width), F32),
            pltpu.VMEM((micro, rows, width), F32),
            pltpu.VMEM((micro, rows, width), BF16),
            pltpu.VMEM((micro, heads, rows, rows), F32),
            pltpu.VMEM((micro, heads, rows, rows), BF16),
            pltpu.VMEM((micro, rows, width), BF16),
            pltpu.VMEM((micro, rows, width), BF16),
            pltpu.VMEM((micro, rows, width), BF16),
            pltpu.VMEM((micro, n_dp, rows, span), BF16),
            pltpu.VMEM((micro, n_mp, rows, width), BF16),
            pltpu.VMEM((micro, 3, rows, width), BF16),
            pltpu.VMEM((micro, 8, rows), F32),
            pltpu.VMEM((micro, 3, 8, rows), F32),
            pltpu.VMEM((slab, span), F32),
            dma((micro, 3)),
            dma((micro, 3)),
            dma((micro,)),
            dma((micro,)),
            dma((micro, n_dp)),
            dma((micro, n_dp)),
            dma((micro, n_dp)),
            dma((micro, n_dp)),
            dma((micro, n_dp)),
            dma((micro, 3)),
            dma((micro, 3)),
            dma((micro, 3)),
            dma((micro, 3)),
            dma((micro,)),
            dma((micro,)),
        ],
        compiler_params=pltpu.CompilerParams(
            collective_id=0, has_side_effects=True, vmem_limit_bytes=50 * 1024 * 1024
        ),
    )(source_rows, value_weight, gate_weight, kernel_weight, segment_ids, out_grad)


def solution(mesh):
    in_specs = (
        P("dp", "mp"),
        P("section", None, "mp"),
        P("section", None, "mp"),
        P("section", None, "mp"),
        P("dp", None),
        P("dp", "mp"),
    )
    out_specs = (P("section", "dp", "mp"), P("section", "dp", "mp"), P("section", "dp", "mp"))
    return jax.shard_map(shards, mesh=mesh, in_specs=in_specs, out_specs=out_specs, check_vma=False)
```

```python
import functools

import jax
import jax.numpy as jnp
from jax import lax
from jax.experimental import pallas as pl
from jax.experimental.pallas import tpu as pltpu
from jax.sharding import PartitionSpec as P

KERNEL = 31
MESH = pl.DeviceIdType.MESH
F32 = jnp.float32
BF16 = jnp.bfloat16


def remote(src, dst, send_sem, recv_sem, device):
    return pltpu.make_async_remote_copy(
        src_ref=src,
        dst_ref=dst,
        send_sem=send_sem,
        recv_sem=recv_sem,
        device_id=device,
        device_id_type=MESH,
    )


def dot(a, b):
    return jnp.dot(a, b, preferred_element_type=F32)


def dot_nt(a, b):
    return lax.dot_general(a, b, (((1,), (1,)), ((), ())), preferred_element_type=F32)


def dot_tn(a, b):
    return lax.dot_general(a, b, (((0,), (0,)), ((), ())), preferred_element_type=F32)


def skew(values, shift):
    fine = shift % 8
    if fine:
        values = pltpu.roll(values, fine, 1)
    return pltpu.roll(values, shift - fine, 1, stride=1, stride_axis=0)


def kernel(
    n_dp,
    micro,
    src_ref,
    wv_hbm,
    wg_hbm,
    wk_hbm,
    seg_hbm,
    og_ref,
    vout_ref,
    gout_ref,
    kout_ref,
    wv_ref,
    wg_ref,
    wk_ref,
    seg_ref,
    xall,
    nf,
    nb,
    invs,
    nt_full,
    nt_all,
    wkp,
    lgs,
    masks,
    vs,
    sigs,
    gateds,
    tps,
    bds,
    bdts,
    hs,
    gbuf,
    gs,
    pairs,
    tails,
    rs_buf,
    rs_in,
    st_buf,
    st_in,
    acc,
    ag_send,
    ag_recv,
    h_send,
    h_recv,
    nt_send,
    nt_recv,
    right_send,
    left_send,
    ring_recv,
    rs_send,
    rs_recv,
    st_send,
    st_recv,
    g_send,
    g_recv,
    load_sem,
):
    d = lax.axis_index("dp")
    s = lax.axis_index("section")
    m = lax.axis_index("mp")
    near = m + 1 - 2 * lax.rem(m, 2)
    across = lax.rem(m + 2, 4)
    corner = lax.rem(near + 2, 4)
    partners = (near, across, corner)
    other = {"section": 1 - s}
    rows = seg_ref.shape[1]
    full, width = wv_ref.shape
    kcols = wk_ref.shape[1]
    heads = kcols // KERNEL
    n_mp = full // width
    slab = full // n_dp
    micros = range(micro)

    lanes = lax.broadcasted_iota(jnp.int32, (rows, rows), 1)
    subs = lax.broadcasted_iota(jnp.int32, (rows, rows), 0)
    offset = lanes - subs + KERNEL // 2
    cyclic = lax.rem(offset + rows, rows) < KERNEL
    low_half = lanes < rows // 2
    flip = jnp.where(lanes + subs == rows - 1, 1.0, 0.0).astype(BF16)

    barrier = pltpu.get_barrier_semaphore()
    for p in partners:
        pl.semaphore_signal(barrier, inc=1, device_id={"mp": p}, device_id_type=MESH)
    pl.semaphore_signal(barrier, inc=1, device_id=other, device_id_type=MESH)

    def greet(i, carry):
        pl.semaphore_signal(
            barrier, inc=1, device_id={"dp": lax.rem(d + i, n_dp)}, device_id_type=MESH
        )
        return carry

    lax.fori_loop(1, n_dp, greet, 0)

    loads = [
        pltpu.make_async_copy(src, dst, load_sem.at[i])
        for i, (src, dst) in enumerate(
            (
                (seg_hbm, seg_ref),
                (wk_hbm.at[0], wk_ref),
                (wv_hbm.at[0], wv_ref),
                (wg_hbm.at[0], wg_ref),
            )
        )
    ]

    def own_load(mb, source, target):
        piece = source.at[pl.ds(mb * rows, rows), :]
        return pltpu.make_async_copy(piece, target, load_sem.at[len(loads) + mb])

    @pl.when(s == 0)
    def _():
        for mb in micros:
            own_load(mb, src_ref, xall.at[mb, m]).start()

    for load in loads:
        load.start()

    @pl.when(s == 1)
    def _():
        for mb in micros:
            own_load(mb, og_ref, gbuf.at[mb]).start()

    pl.semaphore_wait(barrier, 4 + n_dp - 1)

    def gather_copy(mb, rel, first=False):
        block = (m, m, across)[rel]
        target = (near, across, near)[rel]
        source = src_ref.at[pl.ds(mb * rows, rows), :] if first else xall.at[mb, block]
        return remote(
            source,
            xall.at[mb, block],
            ag_send.at[mb, rel],
            ag_recv.at[mb, rel],
            {"mp": target},
        )

    def gather_wait(mb, rel):
        block = (near, across, corner)[rel]
        remote(
            xall.at[mb, block],
            xall.at[mb, block],
            ag_send.at[mb, rel],
            ag_recv.at[mb, rel],
            {"mp": near},
        ).wait_recv()

    def h_copy(mb):
        return remote(hs.at[mb], xall.at[mb, m], h_send.at[mb], h_recv.at[mb], other)

    def g_copy(mb):
        return remote(gs.at[mb], gbuf.at[mb], g_send.at[mb], g_recv.at[mb], other)

    @pl.when(s == 0)
    def _():
        for mb in micros:
            gather_copy(mb, 1, True).start()
            gather_copy(mb, 0, True).start()

    wkp[...] = jnp.zeros_like(wkp)
    acc[...] = jnp.zeros_like(acc)
    loads[0].wait()
    for mb in micros:
        across_seg = jnp.broadcast_to(seg_ref[mb : mb + 1, :].astype(F32), (rows, rows))
        down_seg = jnp.transpose(across_seg)
        same = (across_seg == down_seg) & (offset >= 0) & (offset < KERNEL)
        masks[mb] = jnp.where(same, 1.0, 0.0)
    loads[1].wait()
    wkp[:, :kcols] = wk_ref[...]
    loads[2].wait()
    loads[3].wait()

    @pl.when(s == 0)
    def _():
        for mb in micros:
            own_load(mb, src_ref, xall.at[mb, m]).wait()

    @pl.when(s == 1)
    def _():
        for mb in micros:
            own_load(mb, og_ref, gbuf.at[mb]).wait()

    def gather_start(mb):
        h_copy(mb).wait_recv()
        gather_copy(mb, 1).start()
        gather_copy(mb, 0).start()

    def gather_finish(mb):
        gather_wait(mb, 1)
        gather_copy(mb, 2).start()
        gather_wait(mb, 0)
        gather_wait(mb, 2)

    def forward(mb):
        blocks = [xall[mb, j].astype(F32) for j in range(n_mp)]
        mean = sum(jnp.sum(b, axis=1, keepdims=True) for b in blocks) / full
        centred = [b - mean for b in blocks]
        var = sum(jnp.sum(c * c, axis=1, keepdims=True) for c in centred) / full
        inv = lax.rsqrt(var + 1e-05)
        invs[mb] = jnp.broadcast_to(inv, (rows, rows))
        for j in range(n_mp):
            normed = centred[j] * inv
            nf[mb, j] = normed
            nb[mb, :, j * width : (j + 1) * width] = normed.astype(BF16)
        normed_b = nb[mb]
        lgs[...] = dot(normed_b, wkp[...])
        value = dot(normed_b, wv_ref[...])
        sig = jax.nn.sigmoid(dot(normed_b, wg_ref[...]))
        vs[mb] = value * (1.0 - sig)
        sigs[mb] = sig
        gateds[mb] = (value * sig).astype(BF16)
        logits = lgs[...]
        in_band = masks[mb] > 0.0
        for h in range(heads):
            shift = (rows - KERNEL // 2 - KERNEL * h) % rows
            skewed = skew(logits, shift)
            weights = jnp.where(cyclic, jnp.exp(skewed), 0.0)
            taps = weights / jnp.sum(weights, axis=1, keepdims=True)
            tps[mb, h] = taps
            bds[mb, h] = jnp.where(in_band, taps, 0.0).astype(BF16)

    def mix(mb):
        for p in range(heads // 2):
            cols = slice(p * rows, (p + 1) * rows)
            pair = gateds[mb, :, cols]
            mixed = jnp.where(
                low_half, dot(bds[mb, 2 * p], pair), dot(bds[mb, 2 * p + 1], pair)
            )
            own = xall[mb, m, :, cols].astype(F32)
            hs[mb, :, cols] = (own + mixed).astype(BF16)
        h_copy(mb).start()

    def turn(mb):
        for h in range(heads):
            bdts[mb, h] = jnp.transpose(bds[mb, h])

    def share_normed(mb):
        nt_full[mb] = jnp.transpose(nb[mb])

        def share(i, carry):
            k = lax.rem(d + i, n_dp)
            nt_copy(mb, k).start()
            return carry

        lax.fori_loop(1, n_dp, share, 0)
        nt_all[mb, d] = nt_full[mb, pl.ds(pl.multiple_of(d * slab, slab), slab), :]

    def nt_copy(mb, k):
        return remote(
            nt_full.at[mb, pl.ds(pl.multiple_of(k * slab, slab), slab), :],
            nt_all.at[mb, d],
            nt_send.at[mb, k],
            nt_recv.at[mb, d],
            {"dp": k},
        )

    chunks = range(heads // 2 + 1)

    def chunk(mb, k, c):
        return tails.at[mb, k] if c == heads // 2 else pairs.at[mb, k, c]

    def ring_copy(mb, k, c, step):
        sems = right_send if step == 1 else left_send
        return remote(
            chunk(mb, k, c),
            chunk(mb, k, c),
            sems.at[mb, k, c],
            ring_recv.at[mb, k, c],
            {"dp": d + step},
        )

    def ring_start(mb, k_right, k_left, c):
        @pl.when((d + 1 < n_dp) & (k_right >= 0))
        def _():
            ring_copy(mb, k_right, c, 1).start()

        @pl.when((d > 0) & (k_left < n_dp))
        def _():
            ring_copy(mb, k_left, c, -1).start()

    def backward(mb, eager):
        in_band = masks[mb] > 0.0
        for p in range(heads // 2):
            cols = slice(p * rows, (p + 1) * rows)
            grad_pair = gbuf[mb, :, cols]
            grad_gated = jnp.where(
                low_half,
                dot(bdts[mb, 2 * p], grad_pair),
                dot(bdts[mb, 2 * p + 1], grad_pair),
            )
            grad_value = grad_gated * sigs[mb, :, cols]
            pairs[mb, d, p, :, :rows] = grad_value.astype(BF16)
            pairs[mb, d, p, :, rows:] = (grad_value * vs[mb, :, cols]).astype(BF16)
            if eager:
                ring_start(mb, d, d, p)
        grad_logits = jnp.zeros((rows, rows), F32)
        for p in range(heads // 2):
            cols = slice(p * rows, (p + 1) * rows)
            grad_pair = gbuf[mb, :, cols]
            gated_pair = gateds[mb, :, cols]
            for half in range(2):
                h = 2 * p + half
                keep = low_half if half == 0 else ~low_half
                part = jnp.where(keep, grad_pair.astype(F32), 0.0).astype(BF16)
                grad_taps = jnp.where(in_band, dot_nt(part, gated_pair), 0.0)
                taps = tps[mb, h]
                inner = jnp.sum(taps * grad_taps, axis=1, keepdims=True)
                skewed = (taps * (grad_taps - inner)).astype(BF16)
                shift = (KERNEL // 2 + KERNEL * h + 1) % rows
                grad_logits = grad_logits + skew(dot(flip, skewed), shift)
        tails[mb, d] = dot(flip, grad_logits.astype(BF16)).astype(BF16)
        if eager:
            ring_start(mb, d, d, heads // 2)

    def scatter(mb):
        grad_value = jnp.concatenate([pairs[mb, d, p, :, :rows] for p in range(heads // 2)], axis=1)
        grad_gate = jnp.concatenate([pairs[mb, d, p, :, rows:] for p in range(heads // 2)], axis=1)
        grad_log = tails[mb, d]
        first = jnp.zeros((rows, 1), F32)
        second = jnp.zeros((rows, 1), F32)
        for j in range(n_mp):
            span = slice(j * width, (j + 1) * width)
            part = dot_nt(grad_value, wv_ref[span, :])
            part = part + dot_nt(grad_gate, wg_ref[span, :])
            part = part + dot_nt(grad_log, wkp[span, :])
            rs_buf[mb, j] = part.astype(BF16)
            first = first + jnp.sum(part, axis=1, keepdims=True)
            second = second + jnp.sum(part * nf[mb, j], axis=1, keepdims=True)
        both = jnp.transpose(jnp.where(lanes == 0, first, second))
        st_buf[mb] = both[:8]
        for rel in (1, 2, 0):
            rs_copy(mb, rel).start()
            st_copy(mb, rel).start()
        for c in chunks:
            ring_start(mb, d, d, c)

    def rs_copy(mb, rel):
        return remote(
            rs_buf.at[mb, partners[rel]],
            rs_in.at[mb, rel],
            rs_send.at[mb, rel],
            rs_recv.at[mb, rel],
            {"mp": partners[rel]},
        )

    def st_copy(mb, rel):
        return remote(
            st_buf.at[mb],
            st_in.at[mb, rel],
            st_send.at[mb, rel],
            st_recv.at[mb, rel],
            {"mp": partners[rel]},
        )

    def finish(mb):
        total = rs_buf[mb, m].astype(F32)
        stats = st_buf[mb]
        for rel in range(3):
            rs_copy(mb, rel).wait_recv()
            st_copy(mb, rel).wait_recv()
            total = total + rs_in[mb, rel].astype(F32)
            stats = stats + st_in[mb, rel]
        columns = jnp.transpose(stats) / full
        inv = invs[mb][:, :1]
        grad = inv * (total - columns[:, 0:1] - nf[mb, m] * columns[:, 1:2])
        gs[mb] = (gbuf[mb].astype(F32) + grad).astype(BF16)
        g_copy(mb).start()

    def accumulate(mb, k):
        for c in range(heads // 2):
            acc[c] += dot(nt_all[mb, k], pairs[mb, k, c])
        acc[heads // 2, :, :rows] += dot(nt_all[mb, k], tails[mb, k])

    def ring_step(mb, i):
        left, right = d - i, d + i
        for c in chunks:

            @pl.when(left >= 0)
            def _():
                ring_copy(mb, left, c, -1).wait_recv()

            @pl.when(right < n_dp)
            def _():
                ring_copy(mb, right, c, 1).wait_recv()

            ring_start(mb, left, right, c)
        for k, there in ((left, left >= 0), (right, right < n_dp)):

            @pl.when(there)
            def _():
                remote(
                    nt_all.at[mb, k],
                    nt_all.at[mb, k],
                    nt_send.at[mb, k],
                    nt_recv.at[mb, k],
                    {"dp": k},
                ).wait_recv()
                accumulate(mb, k)

    last = micro - 1

    @pl.when(s == 0)
    def _():
        for mb in micros:
            gather_finish(mb)
            forward(mb)
            mix(mb)
        for mb in micros:
            share_normed(mb)
            turn(mb)
        for mb in micros:
            g_copy(mb).wait_recv()
            backward(mb, True)
            accumulate(mb, d)
            if mb < last:
                ring_step(mb, 1)

    @pl.when(s == 1)
    def _():
        gather_start(0)
        for mb in micros:
            gather_finish(mb)
            forward(mb)
            turn(mb)
            if mb < last:
                gather_start(mb + 1)
            if mb > 0:
                finish(mb - 1)
            backward(mb, False)
            scatter(mb)
            share_normed(mb)
        accumulate(0, d)
        finish(last)
        for mb in range(1, micro):
            accumulate(mb, d)
        for mb in range(last):
            ring_step(mb, 1)

    def ring_round(i, carry):
        for mb in range(last):

            @pl.when(i + 1 < n_dp)
            def _():
                ring_step(mb, i + 1)

        ring_step(last, i)
        return carry

    lax.fori_loop(1, n_dp, ring_round, 0)

    for p in range(heads // 2):
        vout_ref[0, :, p * rows : (p + 1) * rows] = acc[p, :, :rows]
        gout_ref[0, :, p * rows : (p + 1) * rows] = acc[p, :, rows:]
    kout_ref[0] = acc[heads // 2, :, :kcols]

    for mb in micros:
        for rel in range(3):
            gather_copy(mb, rel).wait_send()

        @pl.when(s == 0)
        def _():
            h_copy(mb).wait_send()

        @pl.when(s == 1)
        def _():
            g_copy(mb).wait_send()
            for rel in range(3):
                rs_copy(mb, rel).wait_send()
                st_copy(mb, rel).wait_send()

        def drain(i, carry):
            @pl.when(i > 0)
            def _():
                nt_copy(mb, lax.rem(d + i, n_dp)).wait_send()

            @pl.when((d + 1 < n_dp) & (d - i >= 0))
            def _():
                for c in chunks:
                    ring_copy(mb, d - i, c, 1).wait_send()

            @pl.when((d > 0) & (d + i < n_dp))
            def _():
                for c in chunks:
                    ring_copy(mb, d + i, c, -1).wait_send()

            return carry

        lax.fori_loop(0, n_dp, drain, 0)


def shards(source_rows, value_weight, gate_weight, kernel_weight, segment_ids, out_grad):
    n_dp = lax.axis_size("dp")
    n_mp = lax.axis_size("mp")
    micro, rows = segment_ids.shape
    full, width = value_weight.shape[1:]
    kcols = kernel_weight.shape[2]
    heads = kcols // KERNEL
    slab = full // n_dp
    groups = heads // 2
    vmem = pl.BlockSpec(memory_space=pltpu.VMEM)
    hbm = pl.BlockSpec(memory_space=pltpu.HBM)
    dma = pltpu.SemaphoreType.DMA
    return pl.pallas_call(
        functools.partial(kernel, n_dp, micro),
        out_shape=(
            jax.ShapeDtypeStruct((1, slab, width), F32),
            jax.ShapeDtypeStruct((1, slab, width), F32),
            jax.ShapeDtypeStruct((1, slab, kcols), F32),
        ),
        in_specs=[hbm] * 6,
        out_specs=(vmem, vmem, vmem),
        scratch_shapes=[
            pltpu.VMEM((full, width), BF16),
            pltpu.VMEM((full, width), BF16),
            pltpu.VMEM((full, kcols), BF16),
            pltpu.VMEM((micro, rows), jnp.int32),
            pltpu.VMEM((micro, n_mp, rows, width), BF16),
            pltpu.VMEM((micro, n_mp, rows, width), F32),
            pltpu.VMEM((micro, rows, full), BF16),
            pltpu.VMEM((micro, rows, rows), F32),
            pltpu.VMEM((micro, full, rows), BF16),
            pltpu.VMEM((micro, n_dp, slab, rows), BF16),
            pltpu.VMEM((full, rows), BF16),
            pltpu.VMEM((rows, rows), F32),
            pltpu.VMEM((micro, rows, rows), F32),
            pltpu.VMEM((micro, rows, width), F32),
            pltpu.VMEM((micro, rows, width), F32),
            pltpu.VMEM((micro, rows, width), BF16),
            pltpu.VMEM((micro, heads, rows, rows), F32),
            pltpu.VMEM((micro, heads, rows, rows), BF16),
            pltpu.VMEM((micro, heads, rows, rows), BF16),
            pltpu.VMEM((micro, rows, width), BF16),
            pltpu.VMEM((micro, rows, width), BF16),
            pltpu.VMEM((micro, rows, width), BF16),
            pltpu.VMEM((micro, n_dp, groups, rows, width), BF16),
            pltpu.VMEM((micro, n_dp, rows, rows), BF16),
            pltpu.VMEM((micro, n_mp, rows, width), BF16),
            pltpu.VMEM((micro, 3, rows, width), BF16),
            pltpu.VMEM((micro, 8, rows), F32),
            pltpu.VMEM((micro, 3, 8, rows), F32),
            pltpu.VMEM((groups + 1, slab, width), F32),
            dma((micro, 3)),
            dma((micro, 3)),
            dma((micro,)),
            dma((micro,)),
            dma((micro, n_dp)),
            dma((micro, n_dp)),
            dma((micro, n_dp, groups + 1)),
            dma((micro, n_dp, groups + 1)),
            dma((micro, n_dp, groups + 1)),
            dma((micro, 3)),
            dma((micro, 3)),
            dma((micro, 3)),
            dma((micro, 3)),
            dma((micro,)),
            dma((micro,)),
            dma((4 + micro,)),
        ],
        compiler_params=pltpu.CompilerParams(
            collective_id=0, has_side_effects=True, vmem_limit_bytes=50 * 1024 * 1024
        ),
    )(source_rows, value_weight, gate_weight, kernel_weight, segment_ids, out_grad)


def solution(mesh):
    in_specs = (
        P("dp", "mp"),
        P("section", None, "mp"),
        P("section", None, "mp"),
        P("section", None, "mp"),
        P("dp", None),
        P("dp", "mp"),
    )
    out_specs = (P("section", "dp", "mp"), P("section", "dp", "mp"), P("section", "dp", "mp"))
    return jax.shard_map(shards, mesh=mesh, in_specs=in_specs, out_specs=out_specs, check_vma=False)
```

```python
import functools

import jax
import jax.numpy as jnp
from jax import lax
from jax.experimental import pallas as pl
from jax.experimental.pallas import tpu as pltpu
from jax.sharding import PartitionSpec as P

KERNEL = 31
MESH = pl.DeviceIdType.MESH
F32 = jnp.float32
BF16 = jnp.bfloat16


def remote(src, dst, send_sem, recv_sem, device):
    return pltpu.make_async_remote_copy(
        src_ref=src,
        dst_ref=dst,
        send_sem=send_sem,
        recv_sem=recv_sem,
        device_id=device,
        device_id_type=MESH,
    )


def dot(a, b):
    return jnp.dot(a, b, preferred_element_type=F32)


def dot_nt(a, b):
    return lax.dot_general(a, b, (((1,), (1,)), ((), ())), preferred_element_type=F32)


def dot_tn(a, b):
    return lax.dot_general(a, b, (((0,), (0,)), ((), ())), preferred_element_type=F32)


def skew(values, shift):
    fine = shift % 8
    if fine:
        values = pltpu.roll(values, fine, 1)
    return pltpu.roll(values, shift - fine, 1, stride=1, stride_axis=0)


def kernel(
    n_dp,
    micro,
    src_ref,
    wv_hbm,
    wg_hbm,
    wk_hbm,
    seg_hbm,
    og_ref,
    vout_ref,
    gout_ref,
    kout_ref,
    wv_ref,
    wg_ref,
    wk_ref,
    seg_ref,
    xall,
    nf,
    nb,
    invs,
    nt_full,
    nt_all,
    wkp,
    lgs,
    masks,
    vs,
    sigs,
    gateds,
    tps,
    bds,
    bdts,
    hs,
    gbuf,
    gs,
    pairs,
    tails,
    rs_buf,
    rs_in,
    st_buf,
    st_in,
    acc,
    ag_send,
    ag_recv,
    h_send,
    h_recv,
    nt_send,
    nt_recv,
    right_send,
    left_send,
    ring_recv,
    rs_send,
    rs_recv,
    st_send,
    st_recv,
    g_send,
    g_recv,
    load_sem,
):
    d = lax.axis_index("dp")
    s = lax.axis_index("section")
    m = lax.axis_index("mp")
    near = m + 1 - 2 * lax.rem(m, 2)
    across = lax.rem(m + 2, 4)
    corner = lax.rem(near + 2, 4)
    partners = (near, across, corner)
    other = {"section": 1 - s}
    rows = seg_ref.shape[1]
    full, width = wv_ref.shape
    kcols = wk_ref.shape[1]
    heads = kcols // KERNEL
    n_mp = full // width
    slab = full // n_dp
    micros = range(micro)

    lanes = lax.broadcasted_iota(jnp.int32, (rows, rows), 1)
    subs = lax.broadcasted_iota(jnp.int32, (rows, rows), 0)
    offset = lanes - subs + KERNEL // 2
    cyclic = lax.rem(offset + rows, rows) < KERNEL
    low_half = lanes < rows // 2
    flip = jnp.where(lanes + subs == rows - 1, 1.0, 0.0).astype(BF16)

    barrier = pltpu.get_barrier_semaphore()
    for p in partners:
        pl.semaphore_signal(barrier, inc=1, device_id={"mp": p}, device_id_type=MESH)
    pl.semaphore_signal(barrier, inc=1, device_id=other, device_id_type=MESH)

    def greet(i, carry):
        pl.semaphore_signal(
            barrier, inc=1, device_id={"dp": lax.rem(d + i, n_dp)}, device_id_type=MESH
        )
        return carry

    lax.fori_loop(1, n_dp, greet, 0)

    loads = [
        pltpu.make_async_copy(src, dst, load_sem.at[i])
        for i, (src, dst) in enumerate(
            (
                (seg_hbm, seg_ref),
                (wk_hbm.at[0], wk_ref),
                (wv_hbm.at[0], wv_ref),
                (wg_hbm.at[0], wg_ref),
            )
        )
    ]

    def own_load(mb, source, target):
        piece = source.at[pl.ds(mb * rows, rows), :]
        return pltpu.make_async_copy(piece, target, load_sem.at[len(loads) + mb])

    @pl.when(s == 0)
    def _():
        for mb in micros:
            own_load(mb, src_ref, xall.at[mb, m]).start()

    for load in loads:
        load.start()

    @pl.when(s == 1)
    def _():
        for mb in micros:
            own_load(mb, og_ref, gbuf.at[mb]).start()

    pl.semaphore_wait(barrier, 4 + n_dp - 1)

    def gather_copy(mb, rel, first=False):
        block = (m, m, across)[rel]
        target = (near, across, near)[rel]
        source = src_ref.at[pl.ds(mb * rows, rows), :] if first else xall.at[mb, block]
        return remote(
            source,
            xall.at[mb, block],
            ag_send.at[mb, rel],
            ag_recv.at[mb, rel],
            {"mp": target},
        )

    def gather_wait(mb, rel):
        block = (near, across, corner)[rel]
        remote(
            xall.at[mb, block],
            xall.at[mb, block],
            ag_send.at[mb, rel],
            ag_recv.at[mb, rel],
            {"mp": near},
        ).wait_recv()

    def h_copy(mb):
        return remote(hs.at[mb], xall.at[mb, m], h_send.at[mb], h_recv.at[mb], other)

    def g_copy(mb):
        return remote(gs.at[mb], gbuf.at[mb], g_send.at[mb], g_recv.at[mb], other)

    @pl.when(s == 0)
    def _():
        for mb in micros:
            gather_copy(mb, 1, True).start()
            gather_copy(mb, 0, True).start()

    wkp[...] = jnp.zeros_like(wkp)
    acc[...] = jnp.zeros_like(acc)
    loads[0].wait()
    for mb in micros:
        across_seg = jnp.broadcast_to(seg_ref[mb : mb + 1, :].astype(F32), (rows, rows))
        down_seg = jnp.transpose(across_seg)
        same = (across_seg == down_seg) & (offset >= 0) & (offset < KERNEL)
        masks[mb] = jnp.where(same, 1.0, 0.0)
    loads[1].wait()
    wkp[:, :kcols] = wk_ref[...]
    loads[2].wait()
    loads[3].wait()

    @pl.when(s == 0)
    def _():
        for mb in micros:
            own_load(mb, src_ref, xall.at[mb, m]).wait()

    @pl.when(s == 1)
    def _():
        for mb in micros:
            own_load(mb, og_ref, gbuf.at[mb]).wait()

    def gather_start(mb):
        h_copy(mb).wait_recv()
        gather_copy(mb, 1).start()
        gather_copy(mb, 0).start()

    def gather_finish(mb):
        gather_wait(mb, 1)
        gather_copy(mb, 2).start()
        gather_wait(mb, 0)
        gather_wait(mb, 2)

    def forward(mb):
        blocks = [xall[mb, j].astype(F32) for j in range(n_mp)]
        mean = sum(jnp.sum(b, axis=1, keepdims=True) for b in blocks) / full
        centred = [b - mean for b in blocks]
        var = sum(jnp.sum(c * c, axis=1, keepdims=True) for c in centred) / full
        inv = lax.rsqrt(var + 1e-05)
        invs[mb] = jnp.broadcast_to(inv, (rows, rows))
        for j in range(n_mp):
            normed = centred[j] * inv
            nf[mb, j] = normed
            nb[mb, :, j * width : (j + 1) * width] = normed.astype(BF16)
        normed_b = nb[mb]
        lgs[...] = dot(normed_b, wkp[...])
        value = dot(normed_b, wv_ref[...])
        sig = jax.nn.sigmoid(dot(normed_b, wg_ref[...]))
        vs[mb] = value * (1.0 - sig)
        sigs[mb] = sig
        gateds[mb] = (value * sig).astype(BF16)
        logits = lgs[...]
        in_band = masks[mb] > 0.0
        for h in range(heads):
            shift = (rows - KERNEL // 2 - KERNEL * h) % rows
            skewed = skew(logits, shift)
            weights = jnp.where(cyclic, jnp.exp(skewed), 0.0)
            taps = weights / jnp.sum(weights, axis=1, keepdims=True)
            tps[mb, h] = taps
            bds[mb, h] = jnp.where(in_band, taps, 0.0).astype(BF16)

    def mix(mb):
        for p in range(heads // 2):
            cols = slice(p * rows, (p + 1) * rows)
            pair = gateds[mb, :, cols]
            mixed = jnp.where(
                low_half, dot(bds[mb, 2 * p], pair), dot(bds[mb, 2 * p + 1], pair)
            )
            own = xall[mb, m, :, cols].astype(F32)
            hs[mb, :, cols] = (own + mixed).astype(BF16)
        h_copy(mb).start()

    def turn(mb):
        for h in range(heads):
            bdts[mb, h] = jnp.transpose(bds[mb, h])

    def share_normed(mb):
        nt_full[mb] = jnp.transpose(nb[mb])

        def share(i, carry):
            k = lax.rem(d + i, n_dp)
            nt_copy(mb, k).start()
            return carry

        lax.fori_loop(1, n_dp, share, 0)
        nt_all[mb, d] = nt_full[mb, pl.ds(pl.multiple_of(d * slab, slab), slab), :]

    def nt_copy(mb, k):
        return remote(
            nt_full.at[mb, pl.ds(pl.multiple_of(k * slab, slab), slab), :],
            nt_all.at[mb, d],
            nt_send.at[mb, k],
            nt_recv.at[mb, d],
            {"dp": k},
        )

    chunks = range(heads // 2 + 1)

    def chunk(mb, k, c):
        return tails.at[mb, k] if c == heads // 2 else pairs.at[mb, k, c]

    def ring_copy(mb, k, c, step):
        sems = right_send if step == 1 else left_send
        return remote(
            chunk(mb, k, c),
            chunk(mb, k, c),
            sems.at[mb, k, c],
            ring_recv.at[mb, k, c],
            {"dp": d + step},
        )

    def ring_start(mb, k_right, k_left, c):
        @pl.when((d + 1 < n_dp) & (k_right >= 0))
        def _():
            ring_copy(mb, k_right, c, 1).start()

        @pl.when((d > 0) & (k_left < n_dp))
        def _():
            ring_copy(mb, k_left, c, -1).start()

    def backward(mb, eager):
        in_band = masks[mb] > 0.0
        for p in range(heads // 2):
            cols = slice(p * rows, (p + 1) * rows)
            grad_pair = gbuf[mb, :, cols]
            grad_gated = jnp.where(
                low_half,
                dot(bdts[mb, 2 * p], grad_pair),
                dot(bdts[mb, 2 * p + 1], grad_pair),
            )
            grad_value = grad_gated * sigs[mb, :, cols]
            pairs[mb, d, p, :, :rows] = grad_value.astype(BF16)
            pairs[mb, d, p, :, rows:] = (grad_value * vs[mb, :, cols]).astype(BF16)
            if eager:
                ring_start(mb, d, d, p)
        grad_logits = jnp.zeros((rows, rows), F32)
        for p in range(heads // 2):
            cols = slice(p * rows, (p + 1) * rows)
            grad_pair = gbuf[mb, :, cols]
            gated_pair = gateds[mb, :, cols]
            for half in range(2):
                h = 2 * p + half
                keep = low_half if half == 0 else ~low_half
                part = jnp.where(keep, grad_pair.astype(F32), 0.0).astype(BF16)
                grad_taps = jnp.where(in_band, dot_nt(part, gated_pair), 0.0)
                taps = tps[mb, h]
                inner = jnp.sum(taps * grad_taps, axis=1, keepdims=True)
                skewed = (taps * (grad_taps - inner)).astype(BF16)
                shift = (KERNEL // 2 + KERNEL * h + 1) % rows
                grad_logits = grad_logits + skew(dot(flip, skewed), shift)
        tails[mb, d] = dot(flip, grad_logits.astype(BF16)).astype(BF16)
        if eager:
            ring_start(mb, d, d, heads // 2)

    def scatter(mb):
        grad_value = jnp.concatenate([pairs[mb, d, p, :, :rows] for p in range(heads // 2)], axis=1)
        grad_gate = jnp.concatenate([pairs[mb, d, p, :, rows:] for p in range(heads // 2)], axis=1)
        grad_log = tails[mb, d]
        first = jnp.zeros((rows, 1), F32)
        second = jnp.zeros((rows, 1), F32)
        for j in range(n_mp):
            span = slice(j * width, (j + 1) * width)
            part = dot_nt(grad_value, wv_ref[span, :])
            part = part + dot_nt(grad_gate, wg_ref[span, :])
            part = part + dot_nt(grad_log, wkp[span, :])
            rs_buf[mb, j] = part.astype(BF16)
            first = first + jnp.sum(part, axis=1, keepdims=True)
            second = second + jnp.sum(part * nf[mb, j], axis=1, keepdims=True)
        both = jnp.transpose(jnp.where(lanes == 0, first, second))
        st_buf[mb] = both[:8]
        for rel in (1, 2, 0):
            rs_copy(mb, rel).start()
            st_copy(mb, rel).start()
        for c in chunks:
            ring_start(mb, d, d, c)

    def rs_copy(mb, rel):
        return remote(
            rs_buf.at[mb, partners[rel]],
            rs_in.at[mb, rel],
            rs_send.at[mb, rel],
            rs_recv.at[mb, rel],
            {"mp": partners[rel]},
        )

    def st_copy(mb, rel):
        return remote(
            st_buf.at[mb],
            st_in.at[mb, rel],
            st_send.at[mb, rel],
            st_recv.at[mb, rel],
            {"mp": partners[rel]},
        )

    def finish(mb):
        total = rs_buf[mb, m].astype(F32)
        stats = st_buf[mb]
        for rel in range(3):
            rs_copy(mb, rel).wait_recv()
            st_copy(mb, rel).wait_recv()
            total = total + rs_in[mb, rel].astype(F32)
            stats = stats + st_in[mb, rel]
        columns = jnp.transpose(stats) / full
        inv = invs[mb][:, :1]
        grad = inv * (total - columns[:, 0:1] - nf[mb, m] * columns[:, 1:2])
        gs[mb] = (gbuf[mb].astype(F32) + grad).astype(BF16)
        g_copy(mb).start()

    def accumulate(mb, k):
        for c in range(heads // 2):
            acc[c] += dot(nt_all[mb, k], pairs[mb, k, c])
        acc[heads // 2, :, :rows] += dot(nt_all[mb, k], tails[mb, k])

    def ring_step(mb, i):
        left, right = d - i, d + i
        for c in chunks:

            @pl.when(left >= 0)
            def _():
                ring_copy(mb, left, c, -1).wait_recv()

            @pl.when(right < n_dp)
            def _():
                ring_copy(mb, right, c, 1).wait_recv()

            ring_start(mb, left, right, c)
        for k, there in ((left, left >= 0), (right, right < n_dp)):

            @pl.when(there)
            def _():
                remote(
                    nt_all.at[mb, k],
                    nt_all.at[mb, k],
                    nt_send.at[mb, k],
                    nt_recv.at[mb, k],
                    {"dp": k},
                ).wait_recv()
                accumulate(mb, k)

    last = micro - 1

    @pl.when(s == 0)
    def _():
        for mb in micros:
            gather_finish(mb)
            forward(mb)
            mix(mb)
        for mb in micros:
            share_normed(mb)
            turn(mb)
        for mb in micros:
            g_copy(mb).wait_recv()
            backward(mb, True)
            accumulate(mb, d)
            if mb < last:
                ring_step(mb, 1)

    @pl.when(s == 1)
    def _():
        gather_start(0)
        for mb in micros:
            gather_finish(mb)
            forward(mb)
            turn(mb)
            if mb < last:
                gather_start(mb + 1)
            if mb > 0:
                finish(mb - 1)
            backward(mb, False)
            scatter(mb)
            share_normed(mb)
        accumulate(0, d)
        finish(last)
        for mb in range(1, micro):
            accumulate(mb, d)
        for mb in range(last):
            ring_step(mb, 1)

    def ring_round(i, carry):
        for mb in range(last):

            @pl.when(i + 1 < n_dp)
            def _():
                ring_step(mb, i + 1)

        ring_step(last, i)
        return carry

    lax.fori_loop(1, n_dp, ring_round, 0)

    for p in range(heads // 2):
        vout_ref[0, :, p * rows : (p + 1) * rows] = acc[p, :, :rows]
        gout_ref[0, :, p * rows : (p + 1) * rows] = acc[p, :, rows:]
    turned = jnp.transpose(acc[heads // 2, :, :rows])
    kout_ref[:, 0, :] = turned[:kcols]

    for mb in micros:
        for rel in range(3):
            gather_copy(mb, rel).wait_send()

        @pl.when(s == 0)
        def _():
            h_copy(mb).wait_send()

        @pl.when(s == 1)
        def _():
            g_copy(mb).wait_send()
            for rel in range(3):
                rs_copy(mb, rel).wait_send()
                st_copy(mb, rel).wait_send()

        def drain(i, carry):
            @pl.when(i > 0)
            def _():
                nt_copy(mb, lax.rem(d + i, n_dp)).wait_send()

            @pl.when((d + 1 < n_dp) & (d - i >= 0))
            def _():
                for c in chunks:
                    ring_copy(mb, d - i, c, 1).wait_send()

            @pl.when((d > 0) & (d + i < n_dp))
            def _():
                for c in chunks:
                    ring_copy(mb, d + i, c, -1).wait_send()

            return carry

        lax.fori_loop(0, n_dp, drain, 0)


def deliver(*refs):
    sems = refs[6]
    copies = [pltpu.make_async_copy(refs[i], refs[3 + i], sems.at[i]) for i in range(3)]
    for copy in copies:
        copy.start()
    for copy in copies:
        copy.wait()


def shards(source_rows, value_weight, gate_weight, kernel_weight, segment_ids, out_grad):
    n_dp = lax.axis_size("dp")
    n_mp = lax.axis_size("mp")
    micro, rows = segment_ids.shape
    full, width = value_weight.shape[1:]
    kcols = kernel_weight.shape[2]
    heads = kcols // KERNEL
    slab = full // n_dp
    groups = heads // 2
    vmem = pl.BlockSpec(memory_space=pltpu.VMEM)
    hbm = pl.BlockSpec(memory_space=pltpu.HBM)
    dma = pltpu.SemaphoreType.DMA
    shares = pl.pallas_call(
        functools.partial(kernel, n_dp, micro),
        out_shape=(
            jax.ShapeDtypeStruct((1, slab, width), F32),
            jax.ShapeDtypeStruct((1, slab, width), F32),
            jax.ShapeDtypeStruct((kcols, 1, slab), F32),
        ),
        in_specs=[hbm] * 6,
        out_specs=(vmem, vmem, vmem),
        scratch_shapes=[
            pltpu.VMEM((full, width), BF16),
            pltpu.VMEM((full, width), BF16),
            pltpu.VMEM((full, kcols), BF16),
            pltpu.VMEM((micro, rows), jnp.int32),
            pltpu.VMEM((micro, n_mp, rows, width), BF16),
            pltpu.VMEM((micro, n_mp, rows, width), F32),
            pltpu.VMEM((micro, rows, full), BF16),
            pltpu.VMEM((micro, rows, rows), F32),
            pltpu.VMEM((micro, full, rows), BF16),
            pltpu.VMEM((micro, n_dp, slab, rows), BF16),
            pltpu.VMEM((full, rows), BF16),
            pltpu.VMEM((rows, rows), F32),
            pltpu.VMEM((micro, rows, rows), F32),
            pltpu.VMEM((micro, rows, width), F32),
            pltpu.VMEM((micro, rows, width), F32),
            pltpu.VMEM((micro, rows, width), BF16),
            pltpu.VMEM((micro, heads, rows, rows), F32),
            pltpu.VMEM((micro, heads, rows, rows), BF16),
            pltpu.VMEM((micro, heads, rows, rows), BF16),
            pltpu.VMEM((micro, rows, width), BF16),
            pltpu.VMEM((micro, rows, width), BF16),
            pltpu.VMEM((micro, rows, width), BF16),
            pltpu.VMEM((micro, n_dp, groups, rows, width), BF16),
            pltpu.VMEM((micro, n_dp, rows, rows), BF16),
            pltpu.VMEM((micro, n_mp, rows, width), BF16),
            pltpu.VMEM((micro, 3, rows, width), BF16),
            pltpu.VMEM((micro, 8, rows), F32),
            pltpu.VMEM((micro, 3, 8, rows), F32),
            pltpu.VMEM((groups + 1, slab, width), F32),
            dma((micro, 3)),
            dma((micro, 3)),
            dma((micro,)),
            dma((micro,)),
            dma((micro, n_dp)),
            dma((micro, n_dp)),
            dma((micro, n_dp, groups + 1)),
            dma((micro, n_dp, groups + 1)),
            dma((micro, n_dp, groups + 1)),
            dma((micro, 3)),
            dma((micro, 3)),
            dma((micro, 3)),
            dma((micro, 3)),
            dma((micro,)),
            dma((micro,)),
            dma((4 + micro,)),
        ],
        compiler_params=pltpu.CompilerParams(
            collective_id=0, has_side_effects=True, vmem_limit_bytes=62 * 1024 * 1024
        ),
    )(source_rows, value_weight, gate_weight, kernel_weight, segment_ids, out_grad)
    value_share, gate_share, kernel_share = pl.pallas_call(
        deliver,
        out_shape=tuple(jax.ShapeDtypeStruct(x.shape, x.dtype) for x in shares),
        in_specs=[hbm] * 3,
        out_specs=(hbm,) * 3,
        scratch_shapes=[dma((3,))],
    )(*shares)
    return (value_share, gate_share, jnp.transpose(kernel_share, (1, 2, 0)))


def solution(mesh):
    in_specs = (
        P("dp", "mp"),
        P("section", None, "mp"),
        P("section", None, "mp"),
        P("section", None, "mp"),
        P("dp", None),
        P("dp", "mp"),
    )
    out_specs = (P("section", "dp", "mp"), P("section", "dp", "mp"), P("section", "dp", "mp"))
    return jax.shard_map(shards, mesh=mesh, in_specs=in_specs, out_specs=out_specs, check_vma=False)
```

```python
import functools

import jax
import jax.numpy as jnp
from jax import lax
from jax.experimental import pallas as pl
from jax.experimental.pallas import tpu as pltpu
from jax.sharding import PartitionSpec as P

KERNEL = 31
MESH = pl.DeviceIdType.MESH
F32 = jnp.float32
BF16 = jnp.bfloat16


def remote(src, dst, send_sem, recv_sem, device):
    return pltpu.make_async_remote_copy(
        src_ref=src,
        dst_ref=dst,
        send_sem=send_sem,
        recv_sem=recv_sem,
        device_id=device,
        device_id_type=MESH,
    )


def dot(a, b):
    return jnp.dot(a, b, preferred_element_type=F32)


def dot_nt(a, b):
    return lax.dot_general(a, b, (((1,), (1,)), ((), ())), preferred_element_type=F32)


def dot_tn(a, b):
    return lax.dot_general(a, b, (((0,), (0,)), ((), ())), preferred_element_type=F32)


def skew(values, shift):
    fine = shift % 8
    if fine:
        values = pltpu.roll(values, fine, 1)
    return pltpu.roll(values, shift - fine, 1, stride=1, stride_axis=0)


def kernel(
    n_dp,
    micro,
    src_ref,
    wv_hbm,
    wg_hbm,
    wk_hbm,
    seg_hbm,
    og_ref,
    vout_ref,
    gout_ref,
    kout_ref,
    wv_ref,
    wg_ref,
    wk_ref,
    seg_ref,
    xall,
    nf,
    nb,
    invs,
    nt_full,
    nt_all,
    wkp,
    lgs,
    masks,
    vs,
    sigs,
    gateds,
    tps,
    bds,
    bdts,
    hs,
    gbuf,
    gs,
    pairs,
    tails,
    rs_buf,
    rs_in,
    st_buf,
    st_in,
    acc,
    ag_send,
    ag_recv,
    h_send,
    h_recv,
    nt_send,
    nt_recv,
    right_send,
    left_send,
    ring_recv,
    rs_send,
    rs_recv,
    st_send,
    st_recv,
    g_send,
    g_recv,
    load_sem,
):
    d = lax.axis_index("dp")
    s = lax.axis_index("section")
    m = lax.axis_index("mp")
    near = m + 1 - 2 * lax.rem(m, 2)
    across = lax.rem(m + 2, 4)
    corner = lax.rem(near + 2, 4)
    partners = (near, across, corner)
    other = {"section": 1 - s}
    rows = seg_ref.shape[1]
    full, width = wv_ref.shape
    kcols = wk_ref.shape[1]
    heads = kcols // KERNEL
    n_mp = full // width
    slab = full // n_dp
    micros = range(micro)

    lanes = lax.broadcasted_iota(jnp.int32, (rows, rows), 1)
    subs = lax.broadcasted_iota(jnp.int32, (rows, rows), 0)
    offset = lanes - subs + KERNEL // 2
    cyclic = lax.rem(offset + rows, rows) < KERNEL
    low_half = lanes < rows // 2
    flip = jnp.where(lanes + subs == rows - 1, 1.0, 0.0).astype(BF16)

    barrier = pltpu.get_barrier_semaphore()
    for p in partners:
        pl.semaphore_signal(barrier, inc=1, device_id={"mp": p}, device_id_type=MESH)
    pl.semaphore_signal(barrier, inc=1, device_id=other, device_id_type=MESH)

    def greet(i, carry):
        pl.semaphore_signal(
            barrier, inc=1, device_id={"dp": lax.rem(d + i, n_dp)}, device_id_type=MESH
        )
        return carry

    lax.fori_loop(1, n_dp, greet, 0)

    loads = [
        pltpu.make_async_copy(src, dst, load_sem.at[i])
        for i, (src, dst) in enumerate(
            (
                (seg_hbm, seg_ref),
                (wk_hbm.at[0], wk_ref),
                (wv_hbm.at[0], wv_ref),
                (wg_hbm.at[0], wg_ref),
            )
        )
    ]

    def own_load(mb, source, target):
        piece = source.at[pl.ds(mb * rows, rows), :]
        return pltpu.make_async_copy(piece, target, load_sem.at[len(loads) + mb])

    @pl.when(s == 0)
    def _():
        for mb in micros:
            own_load(mb, src_ref, xall.at[mb, m]).start()

    for load in loads:
        load.start()

    @pl.when(s == 1)
    def _():
        for mb in micros:
            own_load(mb, og_ref, gbuf.at[mb]).start()

    pl.semaphore_wait(barrier, 4 + n_dp - 1)

    def gather_copy(mb, rel, first=False):
        block = (m, m, across)[rel]
        target = (near, across, near)[rel]
        source = src_ref.at[pl.ds(mb * rows, rows), :] if first else xall.at[mb, block]
        return remote(
            source,
            xall.at[mb, block],
            ag_send.at[mb, rel],
            ag_recv.at[mb, rel],
            {"mp": target},
        )

    def gather_wait(mb, rel):
        block = (near, across, corner)[rel]
        remote(
            xall.at[mb, block],
            xall.at[mb, block],
            ag_send.at[mb, rel],
            ag_recv.at[mb, rel],
            {"mp": near},
        ).wait_recv()

    def h_copy(mb):
        return remote(hs.at[mb], xall.at[mb, m], h_send.at[mb], h_recv.at[mb], other)

    def g_copy(mb):
        return remote(gs.at[mb], gbuf.at[mb], g_send.at[mb], g_recv.at[mb], other)

    @pl.when(s == 0)
    def _():
        for mb in micros:
            gather_copy(mb, 1, True).start()
            gather_copy(mb, 0, True).start()

    wkp[...] = jnp.zeros_like(wkp)
    acc[...] = jnp.zeros_like(acc)
    loads[0].wait()
    for mb in micros:
        across_seg = jnp.broadcast_to(seg_ref[mb : mb + 1, :].astype(F32), (rows, rows))
        down_seg = jnp.transpose(across_seg)
        same = (across_seg == down_seg) & (offset >= 0) & (offset < KERNEL)
        masks[mb] = jnp.where(same, 1.0, 0.0)
    loads[1].wait()
    wkp[:, :kcols] = wk_ref[...]
    loads[2].wait()
    loads[3].wait()

    @pl.when(s == 0)
    def _():
        for mb in micros:
            own_load(mb, src_ref, xall.at[mb, m]).wait()

    @pl.when(s == 1)
    def _():
        for mb in micros:
            own_load(mb, og_ref, gbuf.at[mb]).wait()

    def gather_start(mb):
        h_copy(mb).wait_recv()
        gather_copy(mb, 1).start()
        gather_copy(mb, 0).start()

    def gather_finish(mb):
        gather_wait(mb, 1)
        gather_copy(mb, 2).start()
        gather_wait(mb, 0)
        gather_wait(mb, 2)

    def forward(mb):
        blocks = [xall[mb, j].astype(F32) for j in range(n_mp)]
        mean = sum(jnp.sum(b, axis=1, keepdims=True) for b in blocks) / full
        centred = [b - mean for b in blocks]
        var = sum(jnp.sum(c * c, axis=1, keepdims=True) for c in centred) / full
        inv = lax.rsqrt(var + 1e-05)
        invs[mb] = jnp.broadcast_to(inv, (rows, rows))
        for j in range(n_mp):
            normed = centred[j] * inv
            nf[mb, j] = normed
            nb[mb, :, j * width : (j + 1) * width] = normed.astype(BF16)
        normed_b = nb[mb]
        lgs[...] = dot(normed_b, wkp[...])
        value = dot(normed_b, wv_ref[...])
        sig = jax.nn.sigmoid(dot(normed_b, wg_ref[...]))
        vs[mb] = value * (1.0 - sig)
        sigs[mb] = sig
        gateds[mb] = (value * sig).astype(BF16)
        logits = lgs[...]
        in_band = masks[mb] > 0.0
        for h in range(heads):
            shift = (rows - KERNEL // 2 - KERNEL * h) % rows
            skewed = skew(logits, shift)
            weights = jnp.where(cyclic, jnp.exp(skewed), 0.0)
            taps = weights / jnp.sum(weights, axis=1, keepdims=True)
            tps[mb, h] = taps
            bds[mb, h] = jnp.where(in_band, taps, 0.0).astype(BF16)

    def mix(mb):
        for p in range(heads // 2):
            cols = slice(p * rows, (p + 1) * rows)
            pair = gateds[mb, :, cols]
            mixed = jnp.where(
                low_half, dot(bds[mb, 2 * p], pair), dot(bds[mb, 2 * p + 1], pair)
            )
            own = xall[mb, m, :, cols].astype(F32)
            hs[mb, :, cols] = (own + mixed).astype(BF16)
        h_copy(mb).start()

    def turn(mb):
        for h in range(heads):
            bdts[mb, h] = jnp.transpose(bds[mb, h])

    def share_normed(mb):
        nt_full[mb] = jnp.transpose(nb[mb])

        def share(i, carry):
            k = lax.rem(d + i, n_dp)
            nt_copy(mb, k).start()
            return carry

        lax.fori_loop(1, n_dp, share, 0)
        nt_all[mb, d] = nt_full[mb, pl.ds(pl.multiple_of(d * slab, slab), slab), :]

    def nt_copy(mb, k):
        return remote(
            nt_full.at[mb, pl.ds(pl.multiple_of(k * slab, slab), slab), :],
            nt_all.at[mb, d],
            nt_send.at[mb, k],
            nt_recv.at[mb, d],
            {"dp": k},
        )

    chunks = range(heads // 2 + 1)

    def chunk(mb, k, c):
        return tails.at[mb, k] if c == heads // 2 else pairs.at[mb, k, c]

    def ring_copy(mb, k, c, step):
        sems = right_send if step == 1 else left_send
        return remote(
            chunk(mb, k, c),
            chunk(mb, k, c),
            sems.at[mb, k, c],
            ring_recv.at[mb, k, c],
            {"dp": d + step},
        )

    def ring_start(mb, k_right, k_left, c):
        @pl.when((d + 1 < n_dp) & (k_right >= 0))
        def _():
            ring_copy(mb, k_right, c, 1).start()

        @pl.when((d > 0) & (k_left < n_dp))
        def _():
            ring_copy(mb, k_left, c, -1).start()

    def backward(mb, eager):
        in_band = masks[mb] > 0.0
        for p in range(heads // 2):
            cols = slice(p * rows, (p + 1) * rows)
            grad_pair = gbuf[mb, :, cols]
            grad_gated = jnp.where(
                low_half,
                dot(bdts[mb, 2 * p], grad_pair),
                dot(bdts[mb, 2 * p + 1], grad_pair),
            )
            grad_value = grad_gated * sigs[mb, :, cols]
            pairs[mb, d, p, :, :rows] = grad_value.astype(BF16)
            pairs[mb, d, p, :, rows:] = (grad_value * vs[mb, :, cols]).astype(BF16)
            if eager:
                ring_start(mb, d, d, p)
        grad_logits = jnp.zeros((rows, rows), F32)
        for p in range(heads // 2):
            cols = slice(p * rows, (p + 1) * rows)
            grad_pair = gbuf[mb, :, cols]
            gated_pair = gateds[mb, :, cols]
            for half in range(2):
                h = 2 * p + half
                keep = low_half if half == 0 else ~low_half
                part = jnp.where(keep, grad_pair.astype(F32), 0.0).astype(BF16)
                grad_taps = jnp.where(in_band, dot_nt(part, gated_pair), 0.0)
                taps = tps[mb, h]
                inner = jnp.sum(taps * grad_taps, axis=1, keepdims=True)
                skewed = (taps * (grad_taps - inner)).astype(BF16)
                shift = (KERNEL // 2 + KERNEL * h + 1) % rows
                grad_logits = grad_logits + skew(dot(flip, skewed), shift)
        tails[mb, d] = dot(flip, grad_logits.astype(BF16)).astype(BF16)
        if eager:
            ring_start(mb, d, d, heads // 2)

    def scatter(mb):
        grad_value = jnp.concatenate([pairs[mb, d, p, :, :rows] for p in range(heads // 2)], axis=1)
        grad_gate = jnp.concatenate([pairs[mb, d, p, :, rows:] for p in range(heads // 2)], axis=1)
        grad_log = tails[mb, d]
        first = jnp.zeros((rows, 1), F32)
        second = jnp.zeros((rows, 1), F32)
        for j in range(n_mp):
            span = slice(j * width, (j + 1) * width)
            part = dot_nt(grad_value, wv_ref[span, :])
            part = part + dot_nt(grad_gate, wg_ref[span, :])
            part = part + dot_nt(grad_log, wkp[span, :])
            rs_buf[mb, j] = part.astype(BF16)
            first = first + jnp.sum(part, axis=1, keepdims=True)
            second = second + jnp.sum(part * nf[mb, j], axis=1, keepdims=True)
        both = jnp.transpose(jnp.where(lanes == 0, first, second))
        st_buf[mb] = both[:8]
        for rel in (1, 2, 0):
            rs_copy(mb, rel).start()
            st_copy(mb, rel).start()
        for c in chunks:
            ring_start(mb, d, d, c)

    def rs_copy(mb, rel):
        return remote(
            rs_buf.at[mb, partners[rel]],
            rs_in.at[mb, rel],
            rs_send.at[mb, rel],
            rs_recv.at[mb, rel],
            {"mp": partners[rel]},
        )

    def st_copy(mb, rel):
        return remote(
            st_buf.at[mb],
            st_in.at[mb, rel],
            st_send.at[mb, rel],
            st_recv.at[mb, rel],
            {"mp": partners[rel]},
        )

    def finish(mb):
        total = rs_buf[mb, m].astype(F32)
        stats = st_buf[mb]
        for rel in range(3):
            rs_copy(mb, rel).wait_recv()
            st_copy(mb, rel).wait_recv()
            total = total + rs_in[mb, rel].astype(F32)
            stats = stats + st_in[mb, rel]
        columns = jnp.transpose(stats) / full
        inv = invs[mb][:, :1]
        grad = inv * (total - columns[:, 0:1] - nf[mb, m] * columns[:, 1:2])
        gs[mb] = (gbuf[mb].astype(F32) + grad).astype(BF16)
        g_copy(mb).start()

    def accumulate(mb, k):
        for c in range(heads // 2):
            acc[c] += dot(nt_all[mb, k], pairs[mb, k, c])
        acc[heads // 2, :, :rows] += dot(nt_all[mb, k], tails[mb, k])

    def ring_step(mb, i):
        left, right = d - i, d + i
        for c in chunks:

            @pl.when(left >= 0)
            def _():
                ring_copy(mb, left, c, -1).wait_recv()

            @pl.when(right < n_dp)
            def _():
                ring_copy(mb, right, c, 1).wait_recv()

            ring_start(mb, left, right, c)
        for k, there in ((left, left >= 0), (right, right < n_dp)):

            @pl.when(there)
            def _():
                remote(
                    nt_all.at[mb, k],
                    nt_all.at[mb, k],
                    nt_send.at[mb, k],
                    nt_recv.at[mb, k],
                    {"dp": k},
                ).wait_recv()
                accumulate(mb, k)

    last = micro - 1

    @pl.when(s == 0)
    def _():
        for mb in micros:
            gather_finish(mb)
            forward(mb)
            mix(mb)
        for mb in micros:
            share_normed(mb)
            turn(mb)
        for mb in micros:
            g_copy(mb).wait_recv()
            backward(mb, True)
            accumulate(mb, d)
            if mb < last:
                ring_step(mb, 1)

    @pl.when(s == 1)
    def _():
        gather_start(0)
        for mb in micros:
            gather_finish(mb)
            forward(mb)
            turn(mb)
            if mb < last:
                gather_start(mb + 1)
            if mb > 0:
                finish(mb - 1)
            backward(mb, False)
            scatter(mb)
            share_normed(mb)
        accumulate(0, d)
        finish(last)
        for mb in range(1, micro):
            accumulate(mb, d)
        for mb in range(last):
            ring_step(mb, 1)

    def ring_round(i, carry):
        for mb in range(last):

            @pl.when(i + 1 < n_dp)
            def _():
                ring_step(mb, i + 1)

        ring_step(last, i)
        return carry

    lax.fori_loop(1, n_dp, ring_round, 0)

    for p in range(heads // 2):
        vout_ref[0, :, p * rows : (p + 1) * rows] = acc[p, :, :rows]
        gout_ref[0, :, p * rows : (p + 1) * rows] = acc[p, :, rows:]
    turned = jnp.transpose(acc[heads // 2, :, :rows])
    kout_ref[:, 0, :] = turned[:kcols]

    for mb in micros:
        for rel in range(3):
            gather_copy(mb, rel).wait_send()

        @pl.when(s == 0)
        def _():
            h_copy(mb).wait_send()

        @pl.when(s == 1)
        def _():
            g_copy(mb).wait_send()
            for rel in range(3):
                rs_copy(mb, rel).wait_send()
                st_copy(mb, rel).wait_send()

        def drain(i, carry):
            @pl.when(i > 0)
            def _():
                nt_copy(mb, lax.rem(d + i, n_dp)).wait_send()

            @pl.when((d + 1 < n_dp) & (d - i >= 0))
            def _():
                for c in chunks:
                    ring_copy(mb, d - i, c, 1).wait_send()

            @pl.when((d > 0) & (d + i < n_dp))
            def _():
                for c in chunks:
                    ring_copy(mb, d + i, c, -1).wait_send()

            return carry

        lax.fori_loop(0, n_dp, drain, 0)


def deliver(*refs):
    sources, targets, stages, sems = refs[:3], refs[3:6], refs[6:9], refs[9]
    copies = [pltpu.make_async_copy(sources[i], stages[i], sems.at[i]) for i in range(3)]
    for copy in copies:
        copy.start()
    leaving = [pltpu.make_async_copy(stages[i], targets[i], sems.at[3 + i]) for i in range(3)]
    for copy, leave in zip(copies, leaving):
        copy.wait()
        leave.start()
    for leave in leaving:
        leave.wait()


def shards(source_rows, value_weight, gate_weight, kernel_weight, segment_ids, out_grad):
    n_dp = lax.axis_size("dp")
    n_mp = lax.axis_size("mp")
    micro, rows = segment_ids.shape
    full, width = value_weight.shape[1:]
    kcols = kernel_weight.shape[2]
    heads = kcols // KERNEL
    slab = full // n_dp
    groups = heads // 2
    vmem = pl.BlockSpec(memory_space=pltpu.VMEM)
    hbm = pl.BlockSpec(memory_space=pltpu.HBM)
    dma = pltpu.SemaphoreType.DMA
    shares = pl.pallas_call(
        functools.partial(kernel, n_dp, micro),
        out_shape=(
            jax.ShapeDtypeStruct((1, slab, width), F32),
            jax.ShapeDtypeStruct((1, slab, width), F32),
            jax.ShapeDtypeStruct((kcols, 1, slab), F32),
        ),
        in_specs=[hbm] * 6,
        out_specs=(vmem, vmem, vmem),
        scratch_shapes=[
            pltpu.VMEM((full, width), BF16),
            pltpu.VMEM((full, width), BF16),
            pltpu.VMEM((full, kcols), BF16),
            pltpu.VMEM((micro, rows), jnp.int32),
            pltpu.VMEM((micro, n_mp, rows, width), BF16),
            pltpu.VMEM((micro, n_mp, rows, width), F32),
            pltpu.VMEM((micro, rows, full), BF16),
            pltpu.VMEM((micro, rows, rows), F32),
            pltpu.VMEM((micro, full, rows), BF16),
            pltpu.VMEM((micro, n_dp, slab, rows), BF16),
            pltpu.VMEM((full, rows), BF16),
            pltpu.VMEM((rows, rows), F32),
            pltpu.VMEM((micro, rows, rows), F32),
            pltpu.VMEM((micro, rows, width), F32),
            pltpu.VMEM((micro, rows, width), F32),
            pltpu.VMEM((micro, rows, width), BF16),
            pltpu.VMEM((micro, heads, rows, rows), F32),
            pltpu.VMEM((micro, heads, rows, rows), BF16),
            pltpu.VMEM((micro, heads, rows, rows), BF16),
            pltpu.VMEM((micro, rows, width), BF16),
            pltpu.VMEM((micro, rows, width), BF16),
            pltpu.VMEM((micro, rows, width), BF16),
            pltpu.VMEM((micro, n_dp, groups, rows, width), BF16),
            pltpu.VMEM((micro, n_dp, rows, rows), BF16),
            pltpu.VMEM((micro, n_mp, rows, width), BF16),
            pltpu.VMEM((micro, 3, rows, width), BF16),
            pltpu.VMEM((micro, 8, rows), F32),
            pltpu.VMEM((micro, 3, 8, rows), F32),
            pltpu.VMEM((groups + 1, slab, width), F32),
            dma((micro, 3)),
            dma((micro, 3)),
            dma((micro,)),
            dma((micro,)),
            dma((micro, n_dp)),
            dma((micro, n_dp)),
            dma((micro, n_dp, groups + 1)),
            dma((micro, n_dp, groups + 1)),
            dma((micro, n_dp, groups + 1)),
            dma((micro, 3)),
            dma((micro, 3)),
            dma((micro, 3)),
            dma((micro, 3)),
            dma((micro,)),
            dma((micro,)),
            dma((4 + micro,)),
        ],
        compiler_params=pltpu.CompilerParams(
            collective_id=0, has_side_effects=True, vmem_limit_bytes=62 * 1024 * 1024
        ),
    )(source_rows, value_weight, gate_weight, kernel_weight, segment_ids, out_grad)
    value_share, gate_share, kernel_share = pl.pallas_call(
        deliver,
        out_shape=tuple(jax.ShapeDtypeStruct(x.shape, x.dtype) for x in shares),
        in_specs=[hbm] * 3,
        out_specs=(hbm,) * 3,
        scratch_shapes=[pltpu.VMEM(x.shape, x.dtype) for x in shares] + [dma((6,))],
    )(*shares)
    return (value_share, gate_share, jnp.transpose(kernel_share, (1, 2, 0)))


def solution(mesh):
    in_specs = (
        P("dp", "mp"),
        P("section", None, "mp"),
        P("section", None, "mp"),
        P("section", None, "mp"),
        P("dp", None),
        P("dp", "mp"),
    )
    out_specs = (P("section", "dp", "mp"), P("section", "dp", "mp"), P("section", "dp", "mp"))
    return jax.shard_map(shards, mesh=mesh, in_specs=in_specs, out_specs=out_specs, check_vma=False)
```

```python
import functools

import jax
import jax.numpy as jnp
from jax import lax
from jax.experimental import pallas as pl
from jax.experimental.pallas import tpu as pltpu
from jax.sharding import PartitionSpec as P

KERNEL = 31
MESH = pl.DeviceIdType.MESH
F32 = jnp.float32
BF16 = jnp.bfloat16


def remote(src, dst, send_sem, recv_sem, device):
    return pltpu.make_async_remote_copy(
        src_ref=src,
        dst_ref=dst,
        send_sem=send_sem,
        recv_sem=recv_sem,
        device_id=device,
        device_id_type=MESH,
    )


def dot(a, b):
    return jnp.dot(a, b, preferred_element_type=F32)


def dot_nt(a, b):
    return lax.dot_general(a, b, (((1,), (1,)), ((), ())), preferred_element_type=F32)


def dot_tn(a, b):
    return lax.dot_general(a, b, (((0,), (0,)), ((), ())), preferred_element_type=F32)


def skew(values, shift):
    fine = shift % 8
    if fine:
        values = pltpu.roll(values, fine, 1)
    return pltpu.roll(values, shift - fine, 1, stride=1, stride_axis=0)


def kernel(
    n_dp,
    micro,
    src_ref,
    wv_hbm,
    wg_hbm,
    wk_hbm,
    seg_hbm,
    og_ref,
    vout_ref,
    gout_ref,
    kout_ref,
    wv_ref,
    wg_ref,
    wk_ref,
    seg_ref,
    xall,
    nf,
    nb,
    invs,
    nt_full,
    nt_all,
    wkp,
    lgs,
    masks,
    vs,
    sigs,
    gateds,
    tps,
    bds,
    bdts,
    hs,
    gbuf,
    gs,
    pairs,
    tails,
    rs_buf,
    rs_in,
    st_buf,
    st_in,
    acc,
    ag_send,
    ag_recv,
    h_send,
    h_recv,
    nt_send,
    nt_recv,
    right_send,
    left_send,
    ring_recv,
    rs_send,
    rs_recv,
    st_send,
    st_recv,
    g_send,
    g_recv,
    load_sem,
):
    d = lax.axis_index("dp")
    s = lax.axis_index("section")
    m = lax.axis_index("mp")
    near = m + 1 - 2 * lax.rem(m, 2)
    across = lax.rem(m + 2, 4)
    corner = lax.rem(near + 2, 4)
    partners = (near, across, corner)
    other = {"section": 1 - s}
    rows = seg_ref.shape[1]
    full, width = wv_ref.shape
    kcols = wk_ref.shape[1]
    heads = kcols // KERNEL
    n_mp = full // width
    slab = full // n_dp
    micros = range(micro)

    lanes = lax.broadcasted_iota(jnp.int32, (rows, rows), 1)
    subs = lax.broadcasted_iota(jnp.int32, (rows, rows), 0)
    offset = lanes - subs + KERNEL // 2
    cyclic = lax.rem(offset + rows, rows) < KERNEL
    low_half = lanes < rows // 2
    flip = jnp.where(lanes + subs == rows - 1, 1.0, 0.0).astype(BF16)

    barrier = pltpu.get_barrier_semaphore()
    for p in partners:
        pl.semaphore_signal(barrier, inc=1, device_id={"mp": p}, device_id_type=MESH)
    pl.semaphore_signal(barrier, inc=1, device_id=other, device_id_type=MESH)

    def greet(i, carry):
        pl.semaphore_signal(
            barrier, inc=1, device_id={"dp": lax.rem(d + i, n_dp)}, device_id_type=MESH
        )
        return carry

    lax.fori_loop(1, n_dp, greet, 0)

    loads = [
        pltpu.make_async_copy(src, dst, load_sem.at[i])
        for i, (src, dst) in enumerate(
            (
                (seg_hbm, seg_ref),
                (wk_hbm.at[0], wk_ref),
                (wv_hbm.at[0], wv_ref),
                (wg_hbm.at[0], wg_ref),
            )
        )
    ]

    def own_load(mb, source, target):
        piece = source.at[pl.ds(mb * rows, rows), :]
        return pltpu.make_async_copy(piece, target, load_sem.at[len(loads) + mb])

    @pl.when(s == 0)
    def _():
        for mb in micros:
            own_load(mb, src_ref, xall.at[mb, m]).start()

    for load in loads:
        load.start()

    @pl.when(s == 1)
    def _():
        for mb in micros:
            own_load(mb, og_ref, gbuf.at[mb]).start()

    pl.semaphore_wait(barrier, 4 + n_dp - 1)

    def gather_copy(mb, rel, first=False):
        block = (m, m, across)[rel]
        target = (near, across, near)[rel]
        source = src_ref.at[pl.ds(mb * rows, rows), :] if first else xall.at[mb, block]
        return remote(
            source,
            xall.at[mb, block],
            ag_send.at[mb, rel],
            ag_recv.at[mb, rel],
            {"mp": target},
        )

    def gather_wait(mb, rel):
        block = (near, across, corner)[rel]
        remote(
            xall.at[mb, block],
            xall.at[mb, block],
            ag_send.at[mb, rel],
            ag_recv.at[mb, rel],
            {"mp": near},
        ).wait_recv()

    def h_copy(mb):
        return remote(hs.at[mb], xall.at[mb, m], h_send.at[mb], h_recv.at[mb], other)

    def g_copy(mb):
        return remote(gs.at[mb], gbuf.at[mb], g_send.at[mb], g_recv.at[mb], other)

    @pl.when(s == 0)
    def _():
        for mb in micros:
            gather_copy(mb, 1, True).start()
            gather_copy(mb, 0, True).start()

    wkp[...] = jnp.zeros_like(wkp)
    acc[...] = jnp.zeros_like(acc)
    loads[0].wait()
    for mb in micros:
        across_seg = jnp.broadcast_to(seg_ref[mb : mb + 1, :].astype(F32), (rows, rows))
        down_seg = jnp.transpose(across_seg)
        same = (across_seg == down_seg) & (offset >= 0) & (offset < KERNEL)
        masks[mb] = jnp.where(same, 1.0, 0.0)
    loads[1].wait()
    wkp[:, :kcols] = wk_ref[...]
    loads[2].wait()
    loads[3].wait()

    @pl.when(s == 0)
    def _():
        for mb in micros:
            own_load(mb, src_ref, xall.at[mb, m]).wait()

    @pl.when(s == 1)
    def _():
        for mb in micros:
            own_load(mb, og_ref, gbuf.at[mb]).wait()

    def gather_start(mb):
        h_copy(mb).wait_recv()
        gather_copy(mb, 1).start()
        gather_copy(mb, 0).start()

    def gather_finish(mb):
        gather_wait(mb, 1)
        gather_copy(mb, 2).start()
        gather_wait(mb, 0)
        gather_wait(mb, 2)

    def forward(mb):
        blocks = [xall[mb, j].astype(F32) for j in range(n_mp)]
        mean = sum(jnp.sum(b, axis=1, keepdims=True) for b in blocks) / full
        centred = [b - mean for b in blocks]
        var = sum(jnp.sum(c * c, axis=1, keepdims=True) for c in centred) / full
        inv = lax.rsqrt(var + 1e-05)
        invs[mb] = jnp.broadcast_to(inv, (rows, rows))
        for j in range(n_mp):
            normed = centred[j] * inv
            nf[mb, j] = normed
            nb[mb, :, j * width : (j + 1) * width] = normed.astype(BF16)
        normed_b = nb[mb]
        lgs[...] = dot(normed_b, wkp[...])
        value = dot(normed_b, wv_ref[...])
        sig = jax.nn.sigmoid(dot(normed_b, wg_ref[...]))
        vs[mb] = value * (1.0 - sig)
        sigs[mb] = sig
        gateds[mb] = (value * sig).astype(BF16)
        logits = lgs[...]
        in_band = masks[mb] > 0.0
        for h in range(heads):
            shift = (rows - KERNEL // 2 - KERNEL * h) % rows
            skewed = skew(logits, shift)
            weights = jnp.where(cyclic, jnp.exp(skewed), 0.0)
            taps = weights / jnp.sum(weights, axis=1, keepdims=True)
            tps[mb, h] = taps
            bds[mb, h] = jnp.where(in_band, taps, 0.0).astype(BF16)

    def mix(mb):
        for p in range(heads // 2):
            cols = slice(p * rows, (p + 1) * rows)
            pair = gateds[mb, :, cols]
            mixed = jnp.where(
                low_half, dot(bds[mb, 2 * p], pair), dot(bds[mb, 2 * p + 1], pair)
            )
            own = xall[mb, m, :, cols].astype(F32)
            hs[mb, :, cols] = (own + mixed).astype(BF16)
        h_copy(mb).start()

    def turn(mb):
        for h in range(heads):
            bdts[mb, h] = jnp.transpose(bds[mb, h])

    def share_normed(mb):
        nt_full[mb] = jnp.transpose(nb[mb])

        def share(i, carry):
            k = lax.rem(d + i, n_dp)
            nt_copy(mb, k).start()
            return carry

        lax.fori_loop(1, n_dp, share, 0)
        nt_all[mb, d] = nt_full[mb, pl.ds(pl.multiple_of(d * slab, slab), slab), :]

    def nt_copy(mb, k):
        return remote(
            nt_full.at[mb, pl.ds(pl.multiple_of(k * slab, slab), slab), :],
            nt_all.at[mb, d],
            nt_send.at[mb, k],
            nt_recv.at[mb, d],
            {"dp": k},
        )

    chunks = range(heads // 2 + 1)

    def chunk(mb, k, c):
        return tails.at[mb, k] if c == heads // 2 else pairs.at[mb, k, c]

    def ring_copy(mb, k, c, step):
        sems = right_send if step == 1 else left_send
        return remote(
            chunk(mb, k, c),
            chunk(mb, k, c),
            sems.at[mb, k, c],
            ring_recv.at[mb, k, c],
            {"dp": d + step},
        )

    def ring_start(mb, k_right, k_left, c):
        @pl.when((d + 1 < n_dp) & (k_right >= 0))
        def _():
            ring_copy(mb, k_right, c, 1).start()

        @pl.when((d > 0) & (k_left < n_dp))
        def _():
            ring_copy(mb, k_left, c, -1).start()

    def backward(mb, eager):
        in_band = masks[mb] > 0.0
        for p in range(heads // 2):
            cols = slice(p * rows, (p + 1) * rows)
            grad_pair = gbuf[mb, :, cols]
            grad_gated = jnp.where(
                low_half,
                dot(bdts[mb, 2 * p], grad_pair),
                dot(bdts[mb, 2 * p + 1], grad_pair),
            )
            grad_value = grad_gated * sigs[mb, :, cols]
            pairs[mb, d, p, :, :rows] = grad_value.astype(BF16)
            pairs[mb, d, p, :, rows:] = (grad_value * vs[mb, :, cols]).astype(BF16)
            if eager:
                ring_start(mb, d, d, p)
        grad_logits = jnp.zeros((rows, rows), F32)
        for p in range(heads // 2):
            cols = slice(p * rows, (p + 1) * rows)
            grad_pair = gbuf[mb, :, cols]
            gated_pair = gateds[mb, :, cols]
            for half in range(2):
                h = 2 * p + half
                keep = low_half if half == 0 else ~low_half
                part = jnp.where(keep, grad_pair.astype(F32), 0.0).astype(BF16)
                grad_taps = jnp.where(in_band, dot_nt(part, gated_pair), 0.0)
                taps = tps[mb, h]
                inner = jnp.sum(taps * grad_taps, axis=1, keepdims=True)
                skewed = (taps * (grad_taps - inner)).astype(BF16)
                shift = (KERNEL // 2 + KERNEL * h + 1) % rows
                grad_logits = grad_logits + skew(dot(flip, skewed), shift)
        tails[mb, d] = dot(flip, grad_logits.astype(BF16)).astype(BF16)
        if eager:
            ring_start(mb, d, d, heads // 2)

    def scatter(mb):
        grad_value = jnp.concatenate([pairs[mb, d, p, :, :rows] for p in range(heads // 2)], axis=1)
        grad_gate = jnp.concatenate([pairs[mb, d, p, :, rows:] for p in range(heads // 2)], axis=1)
        grad_log = tails[mb, d]
        first = jnp.zeros((rows, 1), F32)
        second = jnp.zeros((rows, 1), F32)
        for j in range(n_mp):
            span = slice(j * width, (j + 1) * width)
            part = dot_nt(grad_value, wv_ref[span, :])
            part = part + dot_nt(grad_gate, wg_ref[span, :])
            part = part + dot_nt(grad_log, wkp[span, :])
            rs_buf[mb, j] = part.astype(BF16)
            first = first + jnp.sum(part, axis=1, keepdims=True)
            second = second + jnp.sum(part * nf[mb, j], axis=1, keepdims=True)
        both = jnp.transpose(jnp.where(lanes == 0, first, second))
        st_buf[mb] = both[:8]
        for rel in (1, 2, 0):
            rs_copy(mb, rel).start()
            st_copy(mb, rel).start()
        for c in chunks:
            ring_start(mb, d, d, c)

    def rs_copy(mb, rel):
        return remote(
            rs_buf.at[mb, partners[rel]],
            rs_in.at[mb, rel],
            rs_send.at[mb, rel],
            rs_recv.at[mb, rel],
            {"mp": partners[rel]},
        )

    def st_copy(mb, rel):
        return remote(
            st_buf.at[mb],
            st_in.at[mb, rel],
            st_send.at[mb, rel],
            st_recv.at[mb, rel],
            {"mp": partners[rel]},
        )

    def finish(mb):
        total = rs_buf[mb, m].astype(F32)
        stats = st_buf[mb]
        for rel in range(3):
            rs_copy(mb, rel).wait_recv()
            st_copy(mb, rel).wait_recv()
            total = total + rs_in[mb, rel].astype(F32)
            stats = stats + st_in[mb, rel]
        columns = jnp.transpose(stats) / full
        inv = invs[mb][:, :1]
        grad = inv * (total - columns[:, 0:1] - nf[mb, m] * columns[:, 1:2])
        gs[mb] = (gbuf[mb].astype(F32) + grad).astype(BF16)
        g_copy(mb).start()

    def accumulate(k):
        for c in range(heads // 2):
            acc[c] += sum(dot(nt_all[mb, k], pairs[mb, k, c]) for mb in micros)
        acc[heads // 2, :, :rows] += sum(dot(nt_all[mb, k], tails[mb, k]) for mb in micros)

    def ring_forward(mb, i):
        left, right = d - i, d + i
        for c in chunks:

            @pl.when(left >= 0)
            def _():
                ring_copy(mb, left, c, -1).wait_recv()

            @pl.when(right < n_dp)
            def _():
                ring_copy(mb, right, c, 1).wait_recv()

            ring_start(mb, left, right, c)

    last = micro - 1

    @pl.when(s == 0)
    def _():
        for mb in micros:
            gather_finish(mb)
            forward(mb)
            mix(mb)
        for mb in micros:
            share_normed(mb)
            turn(mb)
        for mb in micros:
            g_copy(mb).wait_recv()
            backward(mb, True)
            if mb < last:
                ring_forward(mb, 1)

    @pl.when(s == 1)
    def _():
        gather_start(0)
        for mb in micros:
            gather_finish(mb)
            forward(mb)
            turn(mb)
            if mb < last:
                gather_start(mb + 1)
            if mb > 0:
                finish(mb - 1)
            backward(mb, False)
            scatter(mb)
            share_normed(mb)
        for mb in range(last):
            ring_forward(mb, 1)
        finish(last)

    def ring_round(i, carry):
        for mb in range(last):

            @pl.when(i + 1 < n_dp)
            def _():
                ring_forward(mb, i + 1)

        ring_forward(last, i)

        @pl.when(i == 1)
        def _():
            accumulate(d)

        for k, there in ((d - i, d - i >= 0), (d + i, d + i < n_dp)):

            @pl.when(there)
            def _():
                for mb in micros:
                    remote(
                        nt_all.at[mb, k],
                        nt_all.at[mb, k],
                        nt_send.at[mb, k],
                        nt_recv.at[mb, k],
                        {"dp": k},
                    ).wait_recv()
                accumulate(k)

        return carry

    lax.fori_loop(1, n_dp, ring_round, 0)

    for p in range(heads // 2):
        vout_ref[0, :, p * rows : (p + 1) * rows] = acc[p, :, :rows]
        gout_ref[0, :, p * rows : (p + 1) * rows] = acc[p, :, rows:]
    turned = jnp.transpose(acc[heads // 2, :, :rows])
    kout_ref[:, 0, :] = turned[:kcols]

    for mb in micros:
        for rel in range(3):
            gather_copy(mb, rel).wait_send()

        @pl.when(s == 0)
        def _():
            h_copy(mb).wait_send()

        @pl.when(s == 1)
        def _():
            g_copy(mb).wait_send()
            for rel in range(3):
                rs_copy(mb, rel).wait_send()
                st_copy(mb, rel).wait_send()

        def drain(i, carry):
            @pl.when(i > 0)
            def _():
                nt_copy(mb, lax.rem(d + i, n_dp)).wait_send()

            @pl.when((d + 1 < n_dp) & (d - i >= 0))
            def _():
                for c in chunks:
                    ring_copy(mb, d - i, c, 1).wait_send()

            @pl.when((d > 0) & (d + i < n_dp))
            def _():
                for c in chunks:
                    ring_copy(mb, d + i, c, -1).wait_send()

            return carry

        lax.fori_loop(0, n_dp, drain, 0)


def deliver(*refs):
    sources, targets, stages, sems = refs[:3], refs[3:6], refs[6:9], refs[9]
    copies = [pltpu.make_async_copy(sources[i], stages[i], sems.at[i]) for i in range(3)]
    for copy in copies:
        copy.start()
    leaving = [pltpu.make_async_copy(stages[i], targets[i], sems.at[3 + i]) for i in range(3)]
    for copy, leave in zip(copies, leaving):
        copy.wait()
        leave.start()
    for leave in leaving:
        leave.wait()


def shards(source_rows, value_weight, gate_weight, kernel_weight, segment_ids, out_grad):
    n_dp = lax.axis_size("dp")
    n_mp = lax.axis_size("mp")
    micro, rows = segment_ids.shape
    full, width = value_weight.shape[1:]
    kcols = kernel_weight.shape[2]
    heads = kcols // KERNEL
    slab = full // n_dp
    groups = heads // 2
    vmem = pl.BlockSpec(memory_space=pltpu.VMEM)
    hbm = pl.BlockSpec(memory_space=pltpu.HBM)
    dma = pltpu.SemaphoreType.DMA
    shares = pl.pallas_call(
        functools.partial(kernel, n_dp, micro),
        out_shape=(
            jax.ShapeDtypeStruct((1, slab, width), F32),
            jax.ShapeDtypeStruct((1, slab, width), F32),
            jax.ShapeDtypeStruct((kcols, 1, slab), F32),
        ),
        in_specs=[hbm] * 6,
        out_specs=(vmem, vmem, vmem),
        scratch_shapes=[
            pltpu.VMEM((full, width), BF16),
            pltpu.VMEM((full, width), BF16),
            pltpu.VMEM((full, kcols), BF16),
            pltpu.VMEM((micro, rows), jnp.int32),
            pltpu.VMEM((micro, n_mp, rows, width), BF16),
            pltpu.VMEM((micro, n_mp, rows, width), F32),
            pltpu.VMEM((micro, rows, full), BF16),
            pltpu.VMEM((micro, rows, rows), F32),
            pltpu.VMEM((micro, full, rows), BF16),
            pltpu.VMEM((micro, n_dp, slab, rows), BF16),
            pltpu.VMEM((full, rows), BF16),
            pltpu.VMEM((rows, rows), F32),
            pltpu.VMEM((micro, rows, rows), F32),
            pltpu.VMEM((micro, rows, width), F32),
            pltpu.VMEM((micro, rows, width), F32),
            pltpu.VMEM((micro, rows, width), BF16),
            pltpu.VMEM((micro, heads, rows, rows), F32),
            pltpu.VMEM((micro, heads, rows, rows), BF16),
            pltpu.VMEM((micro, heads, rows, rows), BF16),
            pltpu.VMEM((micro, rows, width), BF16),
            pltpu.VMEM((micro, rows, width), BF16),
            pltpu.VMEM((micro, rows, width), BF16),
            pltpu.VMEM((micro, n_dp, groups, rows, width), BF16),
            pltpu.VMEM((micro, n_dp, rows, rows), BF16),
            pltpu.VMEM((micro, n_mp, rows, width), BF16),
            pltpu.VMEM((micro, 3, rows, width), BF16),
            pltpu.VMEM((micro, 8, rows), F32),
            pltpu.VMEM((micro, 3, 8, rows), F32),
            pltpu.VMEM((groups + 1, slab, width), F32),
            dma((micro, 3)),
            dma((micro, 3)),
            dma((micro,)),
            dma((micro,)),
            dma((micro, n_dp)),
            dma((micro, n_dp)),
            dma((micro, n_dp, groups + 1)),
            dma((micro, n_dp, groups + 1)),
            dma((micro, n_dp, groups + 1)),
            dma((micro, 3)),
            dma((micro, 3)),
            dma((micro, 3)),
            dma((micro, 3)),
            dma((micro,)),
            dma((micro,)),
            dma((4 + micro,)),
        ],
        compiler_params=pltpu.CompilerParams(
            collective_id=0, has_side_effects=True, vmem_limit_bytes=62 * 1024 * 1024
        ),
    )(source_rows, value_weight, gate_weight, kernel_weight, segment_ids, out_grad)
    value_share, gate_share, kernel_share = pl.pallas_call(
        deliver,
        out_shape=tuple(jax.ShapeDtypeStruct(x.shape, x.dtype) for x in shares),
        in_specs=[hbm] * 3,
        out_specs=(hbm,) * 3,
        scratch_shapes=[pltpu.VMEM(x.shape, x.dtype) for x in shares] + [dma((6,))],
    )(*shares)
    return (value_share, gate_share, jnp.transpose(kernel_share, (1, 2, 0)))


def solution(mesh):
    in_specs = (
        P("dp", "mp"),
        P("section", None, "mp"),
        P("section", None, "mp"),
        P("section", None, "mp"),
        P("dp", None),
        P("dp", "mp"),
    )
    out_specs = (P("section", "dp", "mp"), P("section", "dp", "mp"), P("section", "dp", "mp"))
    return jax.shard_map(shards, mesh=mesh, in_specs=in_specs, out_specs=out_specs, check_vma=False)
```

```python
import functools

import jax
import jax.numpy as jnp
from jax import lax
from jax.experimental import pallas as pl
from jax.experimental.pallas import tpu as pltpu
from jax.sharding import PartitionSpec as P

KERNEL = 31
MESH = pl.DeviceIdType.MESH
F32 = jnp.float32
BF16 = jnp.bfloat16


def remote(src, dst, send_sem, recv_sem, device):
    return pltpu.make_async_remote_copy(
        src_ref=src,
        dst_ref=dst,
        send_sem=send_sem,
        recv_sem=recv_sem,
        device_id=device,
        device_id_type=MESH,
    )


def dot(a, b):
    return jnp.dot(a, b, preferred_element_type=F32)


def dot_nt(a, b):
    return lax.dot_general(a, b, (((1,), (1,)), ((), ())), preferred_element_type=F32)


def dot_tn(a, b):
    return lax.dot_general(a, b, (((0,), (0,)), ((), ())), preferred_element_type=F32)


def skew(values, shift):
    fine = shift % 8
    if fine:
        values = pltpu.roll(values, fine, 1)
    return pltpu.roll(values, shift - fine, 1, stride=1, stride_axis=0)


def kernel(
    n_dp,
    micro,
    src_ref,
    wv_hbm,
    wg_hbm,
    wk_hbm,
    seg_hbm,
    og_ref,
    vout_ref,
    gout_ref,
    kout_ref,
    wv_ref,
    wg_ref,
    wk_ref,
    seg_ref,
    xall,
    nf,
    nb,
    invs,
    nt_full,
    nt_all,
    wkp,
    lgs,
    masks,
    vs,
    sigs,
    gateds,
    tps,
    bds,
    bdts,
    hs,
    gbuf,
    gs,
    pairs,
    tails,
    rs_buf,
    rs_in,
    st_buf,
    st_in,
    acc,
    ag_send,
    ag_recv,
    h_send,
    h_recv,
    nt_send,
    nt_recv,
    right_send,
    left_send,
    ring_recv,
    rs_send,
    rs_recv,
    st_send,
    st_recv,
    g_send,
    g_recv,
    load_sem,
):
    d = lax.axis_index("dp")
    s = lax.axis_index("section")
    m = lax.axis_index("mp")
    near = m + 1 - 2 * lax.rem(m, 2)
    across = lax.rem(m + 2, 4)
    corner = lax.rem(near + 2, 4)
    partners = (near, across, corner)
    other = {"section": 1 - s}
    rows = seg_ref.shape[1]
    full, width = wv_ref.shape
    kcols = wk_ref.shape[1]
    heads = kcols // KERNEL
    n_mp = full // width
    slab = full // n_dp
    micros = range(micro)

    lanes = lax.broadcasted_iota(jnp.int32, (rows, rows), 1)
    subs = lax.broadcasted_iota(jnp.int32, (rows, rows), 0)
    offset = lanes - subs + KERNEL // 2
    cyclic = lax.rem(offset + rows, rows) < KERNEL
    low_half = lanes < rows // 2
    flip = jnp.where(lanes + subs == rows - 1, 1.0, 0.0).astype(BF16)

    barrier = pltpu.get_barrier_semaphore()
    for p in partners:
        pl.semaphore_signal(barrier, inc=1, device_id={"mp": p}, device_id_type=MESH)
    pl.semaphore_signal(barrier, inc=1, device_id=other, device_id_type=MESH)

    def greet(i, carry):
        pl.semaphore_signal(
            barrier, inc=1, device_id={"dp": lax.rem(d + i, n_dp)}, device_id_type=MESH
        )
        return carry

    lax.fori_loop(1, n_dp, greet, 0)

    loads = [
        pltpu.make_async_copy(src, dst, load_sem.at[i])
        for i, (src, dst) in enumerate(
            (
                (seg_hbm, seg_ref),
                (wk_hbm.at[0], wk_ref),
                (wv_hbm.at[0], wv_ref),
                (wg_hbm.at[0], wg_ref),
            )
        )
    ]

    def own_load(mb, source, target):
        piece = source.at[pl.ds(mb * rows, rows), :]
        return pltpu.make_async_copy(piece, target, load_sem.at[len(loads) + mb])

    @pl.when(s == 0)
    def _():
        for mb in micros:
            own_load(mb, src_ref, xall.at[mb, m]).start()

    for load in loads:
        load.start()

    @pl.when(s == 1)
    def _():
        for mb in micros:
            own_load(mb, og_ref, gbuf.at[mb]).start()

    pl.semaphore_wait(barrier, 4 + n_dp - 1)

    def gather_copy(mb, rel, first=False):
        block = (m, m, across)[rel]
        target = (near, across, near)[rel]
        source = src_ref.at[pl.ds(mb * rows, rows), :] if first else xall.at[mb, block]
        return remote(
            source,
            xall.at[mb, block],
            ag_send.at[mb, rel],
            ag_recv.at[mb, rel],
            {"mp": target},
        )

    def gather_wait(mb, rel):
        block = (near, across, corner)[rel]
        remote(
            xall.at[mb, block],
            xall.at[mb, block],
            ag_send.at[mb, rel],
            ag_recv.at[mb, rel],
            {"mp": near},
        ).wait_recv()

    def h_copy(mb):
        return remote(hs.at[mb], xall.at[mb, m], h_send.at[mb], h_recv.at[mb], other)

    def g_copy(mb):
        return remote(gs.at[mb], gbuf.at[mb], g_send.at[mb], g_recv.at[mb], other)

    @pl.when(s == 0)
    def _():
        for mb in micros:
            gather_copy(mb, 1, True).start()
            gather_copy(mb, 0, True).start()

    wkp[...] = jnp.zeros_like(wkp)
    acc[...] = jnp.zeros_like(acc)
    loads[0].wait()
    for mb in micros:
        across_seg = jnp.broadcast_to(seg_ref[mb : mb + 1, :].astype(F32), (rows, rows))
        down_seg = jnp.transpose(across_seg)
        same = (across_seg == down_seg) & (offset >= 0) & (offset < KERNEL)
        masks[mb] = jnp.where(same, 1.0, 0.0)
    loads[1].wait()
    wkp[:, :kcols] = wk_ref[...]
    loads[2].wait()
    loads[3].wait()

    @pl.when(s == 0)
    def _():
        for mb in micros:
            own_load(mb, src_ref, xall.at[mb, m]).wait()

    @pl.when(s == 1)
    def _():
        for mb in micros:
            own_load(mb, og_ref, gbuf.at[mb]).wait()

    def gather_start(mb):
        h_copy(mb).wait_recv()
        gather_copy(mb, 1).start()
        gather_copy(mb, 0).start()

    def gather_finish(mb):
        gather_wait(mb, 1)
        gather_copy(mb, 2).start()
        gather_wait(mb, 0)
        gather_wait(mb, 2)

    def forward(mb):
        blocks = [xall[mb, j].astype(F32) for j in range(n_mp)]
        mean = sum(jnp.sum(b, axis=1, keepdims=True) for b in blocks) / full
        centred = [b - mean for b in blocks]
        var = sum(jnp.sum(c * c, axis=1, keepdims=True) for c in centred) / full
        inv = lax.rsqrt(var + 1e-05)
        invs[mb] = jnp.broadcast_to(inv, (rows, rows))
        for j in range(n_mp):
            normed = centred[j] * inv
            nf[mb, j] = normed
            nb[mb, :, j * width : (j + 1) * width] = normed.astype(BF16)
        normed_b = nb[mb]
        lgs[...] = dot(normed_b, wkp[...])
        value = dot(normed_b, wv_ref[...])
        sig = jax.nn.sigmoid(dot(normed_b, wg_ref[...]))
        vs[mb] = value * (1.0 - sig)
        sigs[mb] = sig
        gateds[mb] = (value * sig).astype(BF16)
        logits = lgs[...]
        in_band = masks[mb] > 0.0
        for h in range(heads):
            shift = (rows - KERNEL // 2 - KERNEL * h) % rows
            skewed = skew(logits, shift)
            weights = jnp.where(cyclic, jnp.exp(skewed), 0.0)
            taps = weights / jnp.sum(weights, axis=1, keepdims=True)
            tps[mb, h] = taps
            bds[mb, h] = jnp.where(in_band, taps, 0.0).astype(BF16)

    def mix(mb):
        for p in range(heads // 2):
            cols = slice(p * rows, (p + 1) * rows)
            pair = gateds[mb, :, cols]
            mixed = jnp.where(
                low_half, dot(bds[mb, 2 * p], pair), dot(bds[mb, 2 * p + 1], pair)
            )
            own = xall[mb, m, :, cols].astype(F32)
            hs[mb, :, cols] = (own + mixed).astype(BF16)
        h_copy(mb).start()

    def turn(mb):
        for h in range(heads):
            bdts[mb, h] = jnp.transpose(bds[mb, h])

    def share_normed(mb):
        nt_full[mb] = jnp.transpose(nb[mb])

        def share(i, carry):
            k = lax.rem(d + i, n_dp)
            nt_copy(mb, k).start()
            return carry

        lax.fori_loop(1, n_dp, share, 0)
        nt_all[mb, d] = nt_full[mb, pl.ds(pl.multiple_of(d * slab, slab), slab), :]

    def nt_copy(mb, k):
        return remote(
            nt_full.at[mb, pl.ds(pl.multiple_of(k * slab, slab), slab), :],
            nt_all.at[mb, d],
            nt_send.at[mb, k],
            nt_recv.at[mb, d],
            {"dp": k},
        )

    chunks = range(heads // 2 + 1)

    def chunk(mb, k, c):
        return tails.at[mb, k] if c == heads // 2 else pairs.at[mb, k, c]

    def ring_copy(mb, k, c, step):
        sems = right_send if step == 1 else left_send
        return remote(
            chunk(mb, k, c),
            chunk(mb, k, c),
            sems.at[mb, k, c],
            ring_recv.at[mb, k, c],
            {"dp": d + step},
        )

    def ring_start(mb, k_right, k_left, c):
        @pl.when((d + 1 < n_dp) & (k_right >= 0))
        def _():
            ring_copy(mb, k_right, c, 1).start()

        @pl.when((d > 0) & (k_left < n_dp))
        def _():
            ring_copy(mb, k_left, c, -1).start()

    def backward(mb, eager):
        in_band = masks[mb] > 0.0
        for p in range(heads // 2):
            cols = slice(p * rows, (p + 1) * rows)
            grad_pair = gbuf[mb, :, cols]
            grad_gated = jnp.where(
                low_half,
                dot(bdts[mb, 2 * p], grad_pair),
                dot(bdts[mb, 2 * p + 1], grad_pair),
            )
            grad_value = grad_gated * sigs[mb, :, cols]
            pairs[mb, d, p, :, :rows] = grad_value.astype(BF16)
            pairs[mb, d, p, :, rows:] = (grad_value * vs[mb, :, cols]).astype(BF16)
            if eager:
                ring_start(mb, d, d, p)
        grad_logits = jnp.zeros((rows, rows), F32)
        for p in range(heads // 2):
            cols = slice(p * rows, (p + 1) * rows)
            grad_pair = gbuf[mb, :, cols]
            gated_pair = gateds[mb, :, cols]
            for half in range(2):
                h = 2 * p + half
                keep = low_half if half == 0 else ~low_half
                part = jnp.where(keep, grad_pair.astype(F32), 0.0).astype(BF16)
                grad_taps = jnp.where(in_band, dot_nt(part, gated_pair), 0.0)
                taps = tps[mb, h]
                inner = jnp.sum(taps * grad_taps, axis=1, keepdims=True)
                skewed = (taps * (grad_taps - inner)).astype(BF16)
                shift = (KERNEL // 2 + KERNEL * h + 1) % rows
                grad_logits = grad_logits + skew(dot(flip, skewed), shift)
        tails[mb, d] = dot(flip, grad_logits.astype(BF16)).astype(BF16)
        if eager:
            ring_start(mb, d, d, heads // 2)

    def scatter(mb):
        grad_value = jnp.concatenate([pairs[mb, d, p, :, :rows] for p in range(heads // 2)], axis=1)
        grad_gate = jnp.concatenate([pairs[mb, d, p, :, rows:] for p in range(heads // 2)], axis=1)
        grad_log = tails[mb, d]
        first = jnp.zeros((rows, 1), F32)
        second = jnp.zeros((rows, 1), F32)
        for j in range(n_mp):
            span = slice(j * width, (j + 1) * width)
            part = dot_nt(grad_value, wv_ref[span, :])
            part = part + dot_nt(grad_gate, wg_ref[span, :])
            part = part + dot_nt(grad_log, wkp[span, :])
            rs_buf[mb, j] = part.astype(BF16)
            first = first + jnp.sum(part, axis=1, keepdims=True)
            second = second + jnp.sum(part * nf[mb, j], axis=1, keepdims=True)
        both = jnp.transpose(jnp.where(lanes == 0, first, second))
        st_buf[mb] = both[:8]
        for rel in (1, 2, 0):
            rs_copy(mb, rel).start()
            st_copy(mb, rel).start()
        for c in chunks:
            ring_start(mb, d, d, c)

    def rs_copy(mb, rel):
        return remote(
            rs_buf.at[mb, partners[rel]],
            rs_in.at[mb, rel],
            rs_send.at[mb, rel],
            rs_recv.at[mb, rel],
            {"mp": partners[rel]},
        )

    def st_copy(mb, rel):
        return remote(
            st_buf.at[mb],
            st_in.at[mb, rel],
            st_send.at[mb, rel],
            st_recv.at[mb, rel],
            {"mp": partners[rel]},
        )

    def finish(mb):
        total = rs_buf[mb, m].astype(F32)
        stats = st_buf[mb]
        for rel in range(3):
            rs_copy(mb, rel).wait_recv()
            st_copy(mb, rel).wait_recv()
            total = total + rs_in[mb, rel].astype(F32)
            stats = stats + st_in[mb, rel]
        columns = jnp.transpose(stats) / full
        inv = invs[mb][:, :1]
        grad = inv * (total - columns[:, 0:1] - nf[mb, m] * columns[:, 1:2])
        gs[mb] = (gbuf[mb].astype(F32) + grad).astype(BF16)
        g_copy(mb).start()

    def accumulate(k):
        for c in range(heads // 2):
            acc[c] += sum(dot(nt_all[mb, k], pairs[mb, k, c]) for mb in micros)
        acc[heads // 2, :, :rows] += sum(dot(nt_all[mb, k], tails[mb, k]) for mb in micros)

    def ring_forward(mb, i):
        left, right = d - i, d + i
        for c in chunks:

            @pl.when(left >= 0)
            def _():
                ring_copy(mb, left, c, -1).wait_recv()

            @pl.when(right < n_dp)
            def _():
                ring_copy(mb, right, c, 1).wait_recv()

            ring_start(mb, left, right, c)

    last = micro - 1

    @pl.when(s == 0)
    def _():
        for mb in micros:
            gather_finish(mb)
            forward(mb)
            mix(mb)
        for mb in micros:
            share_normed(mb)
            turn(mb)
        for mb in micros:
            g_copy(mb).wait_recv()
            backward(mb, True)
            if mb < last:
                ring_forward(mb, 1)

    @pl.when(s == 1)
    def _():
        gather_start(0)
        for mb in micros:
            gather_finish(mb)
            forward(mb)
            turn(mb)
            if mb < last:
                gather_start(mb + 1)
            if mb > 0:
                finish(mb - 1)
            share_normed(mb)
            backward(mb, False)
            scatter(mb)
        for mb in range(last):
            ring_forward(mb, 1)
        finish(last)

    def ring_round(i, carry):
        for mb in range(last):

            @pl.when(i + 1 < n_dp)
            def _():
                ring_forward(mb, i + 1)

        ring_forward(last, i)

        @pl.when(i == 1)
        def _():
            accumulate(d)

        for k, there in ((d - i, d - i >= 0), (d + i, d + i < n_dp)):

            @pl.when(there)
            def _():
                for mb in micros:
                    remote(
                        nt_all.at[mb, k],
                        nt_all.at[mb, k],
                        nt_send.at[mb, k],
                        nt_recv.at[mb, k],
                        {"dp": k},
                    ).wait_recv()
                accumulate(k)

        return carry

    lax.fori_loop(1, n_dp, ring_round, 0)

    for p in range(heads // 2):
        vout_ref[0, :, p * rows : (p + 1) * rows] = acc[p, :, :rows]
        gout_ref[0, :, p * rows : (p + 1) * rows] = acc[p, :, rows:]
    turned = jnp.transpose(acc[heads // 2, :, :rows])
    kout_ref[:, 0, :] = turned[:kcols]

    for mb in micros:
        for rel in range(3):
            gather_copy(mb, rel).wait_send()

        @pl.when(s == 0)
        def _():
            h_copy(mb).wait_send()

        @pl.when(s == 1)
        def _():
            g_copy(mb).wait_send()
            for rel in range(3):
                rs_copy(mb, rel).wait_send()
                st_copy(mb, rel).wait_send()

        def drain(i, carry):
            @pl.when(i > 0)
            def _():
                nt_copy(mb, lax.rem(d + i, n_dp)).wait_send()

            @pl.when((d + 1 < n_dp) & (d - i >= 0))
            def _():
                for c in chunks:
                    ring_copy(mb, d - i, c, 1).wait_send()

            @pl.when((d > 0) & (d + i < n_dp))
            def _():
                for c in chunks:
                    ring_copy(mb, d + i, c, -1).wait_send()

            return carry

        lax.fori_loop(0, n_dp, drain, 0)


def deliver(*refs):
    sources, targets, stages, sems = refs[:3], refs[3:6], refs[6:9], refs[9]
    copies = [pltpu.make_async_copy(sources[i], stages[i], sems.at[i]) for i in range(3)]
    for copy in copies:
        copy.start()
    leaving = [pltpu.make_async_copy(stages[i], targets[i], sems.at[3 + i]) for i in range(3)]
    for copy, leave in zip(copies, leaving):
        copy.wait()
        leave.start()
    for leave in leaving:
        leave.wait()


def shards(source_rows, value_weight, gate_weight, kernel_weight, segment_ids, out_grad):
    n_dp = lax.axis_size("dp")
    n_mp = lax.axis_size("mp")
    micro, rows = segment_ids.shape
    full, width = value_weight.shape[1:]
    kcols = kernel_weight.shape[2]
    heads = kcols // KERNEL
    slab = full // n_dp
    groups = heads // 2
    vmem = pl.BlockSpec(memory_space=pltpu.VMEM)
    hbm = pl.BlockSpec(memory_space=pltpu.HBM)
    dma = pltpu.SemaphoreType.DMA
    shares = pl.pallas_call(
        functools.partial(kernel, n_dp, micro),
        out_shape=(
            jax.ShapeDtypeStruct((1, slab, width), F32),
            jax.ShapeDtypeStruct((1, slab, width), F32),
            jax.ShapeDtypeStruct((kcols, 1, slab), F32),
        ),
        in_specs=[hbm] * 6,
        out_specs=(vmem, vmem, vmem),
        scratch_shapes=[
            pltpu.VMEM((full, width), BF16),
            pltpu.VMEM((full, width), BF16),
            pltpu.VMEM((full, kcols), BF16),
            pltpu.VMEM((micro, rows), jnp.int32),
            pltpu.VMEM((micro, n_mp, rows, width), BF16),
            pltpu.VMEM((micro, n_mp, rows, width), F32),
            pltpu.VMEM((micro, rows, full), BF16),
            pltpu.VMEM((micro, rows, rows), F32),
            pltpu.VMEM((micro, full, rows), BF16),
            pltpu.VMEM((micro, n_dp, slab, rows), BF16),
            pltpu.VMEM((full, rows), BF16),
            pltpu.VMEM((rows, rows), F32),
            pltpu.VMEM((micro, rows, rows), F32),
            pltpu.VMEM((micro, rows, width), F32),
            pltpu.VMEM((micro, rows, width), F32),
            pltpu.VMEM((micro, rows, width), BF16),
            pltpu.VMEM((micro, heads, rows, rows), F32),
            pltpu.VMEM((micro, heads, rows, rows), BF16),
            pltpu.VMEM((micro, heads, rows, rows), BF16),
            pltpu.VMEM((micro, rows, width), BF16),
            pltpu.VMEM((micro, rows, width), BF16),
            pltpu.VMEM((micro, rows, width), BF16),
            pltpu.VMEM((micro, n_dp, groups, rows, width), BF16),
            pltpu.VMEM((micro, n_dp, rows, rows), BF16),
            pltpu.VMEM((micro, n_mp, rows, width), BF16),
            pltpu.VMEM((micro, 3, rows, width), BF16),
            pltpu.VMEM((micro, 8, rows), F32),
            pltpu.VMEM((micro, 3, 8, rows), F32),
            pltpu.VMEM((groups + 1, slab, width), F32),
            dma((micro, 3)),
            dma((micro, 3)),
            dma((micro,)),
            dma((micro,)),
            dma((micro, n_dp)),
            dma((micro, n_dp)),
            dma((micro, n_dp, groups + 1)),
            dma((micro, n_dp, groups + 1)),
            dma((micro, n_dp, groups + 1)),
            dma((micro, 3)),
            dma((micro, 3)),
            dma((micro, 3)),
            dma((micro, 3)),
            dma((micro,)),
            dma((micro,)),
            dma((4 + micro,)),
        ],
        compiler_params=pltpu.CompilerParams(
            collective_id=0, has_side_effects=True, vmem_limit_bytes=62 * 1024 * 1024
        ),
    )(source_rows, value_weight, gate_weight, kernel_weight, segment_ids, out_grad)
    value_share, gate_share, kernel_share = pl.pallas_call(
        deliver,
        out_shape=tuple(jax.ShapeDtypeStruct(x.shape, x.dtype) for x in shares),
        in_specs=[hbm] * 3,
        out_specs=(hbm,) * 3,
        scratch_shapes=[pltpu.VMEM(x.shape, x.dtype) for x in shares] + [dma((6,))],
    )(*shares)
    return (value_share, gate_share, jnp.transpose(kernel_share, (1, 2, 0)))


def solution(mesh):
    in_specs = (
        P("dp", "mp"),
        P("section", None, "mp"),
        P("section", None, "mp"),
        P("section", None, "mp"),
        P("dp", None),
        P("dp", "mp"),
    )
    out_specs = (P("section", "dp", "mp"), P("section", "dp", "mp"), P("section", "dp", "mp"))
    return jax.shard_map(shards, mesh=mesh, in_specs=in_specs, out_specs=out_specs, check_vma=False)
```
